512 devices in a mesh: heads: 8 (over z), ctx: 64 (over y, x, core).
Axes of the slice: x: 4, y: 8, z: 8, core: 2. Of those that a mesh axis runs over, the one named last changes fastest.
Arguments:
- queries: bfloat16 [8, 8192, 512], P('heads', 'ctx'), may hold values from -16 to 16
- keys: bfloat16 [8, 8192, 128], P('heads', 'ctx'), may hold values from -16 to 16
- values: bfloat16 [8, 8192, 128], P('heads', 'ctx'), may hold values from -43 to 43
- out_grad: bfloat16 [8, 8192, 512], P('heads', 'ctx'), may hold values from -43 to 43
- gain_lin: float32 [8, 512], P('heads'), may hold values from 0.1 to 1.9
- gain_sparse: float32 [8, 512], P('heads'), may hold values from 0.1 to 1.9
- key_blocks: int32 [8, 64, 4], P('heads'), may hold values from -1 to 63, as said below
- w_feat: bfloat16 [128, 256], replicated, may hold values from -0.5 to 0.5
Outputs:
- query_grads: bfloat16 [8, 8192, 512], P('heads', 'ctx')
- key_grads: bfloat16 [8, 8192, 128], P('heads', 'ctx')
- value_grads: bfloat16 [8, 8192, 128], P('heads', 'ctx')
- w_grad: float32 [128, 256], replicated
The draws below stay inside these ranges and needn't reach their ends.
Inputs may be any that keep to these rules, and one draw needn't show every extreme that they name: `key_blocks`: entry r - 1 of row i for head group g is -1 or the index of a key block of context shard i - r (r = 1 to 4): a shard takes at most one block from each of the 4 shards before it, and -1 stands where it takes none or i - r < 0. Counts differ from shard to shard; in every head group some shard takes a block from all 4 preceding shards, and some shard gives a block to all 4 shards after it.
All inputs are finite; a program needn't handle non-finite values.
Results may differ from the reference program's by a relative error of at most 0.009.
Values may be sent and summed in bfloat16 or wider, within the bound.
No kernel may reach another device: no remote copies, remote signals or barrier semaphores. Data moves between devices by JAX's collectives and lax.ppermute only.
A program may use at most 64 MiB of HBM per device.

```python
import jax
import jax.numpy as jnp
from jax import lax

DH = 128
GQ = 4
F = 256
BLK = 128
R = 4
TOK_DEV = 128
KVH = 8
TOKENS = 8192
BPS = 1
NBLK = 64


def draw_queries(key, part):
    own_key = jax.random.fold_in(key, 11)
    shape = (KVH, TOKENS, GQ * DH)
    field = jnp.clip(jax.random.normal(own_key, shape, jnp.float32), -4.0, 4.0)
    return field.astype(jnp.bfloat16)


def draw_keys(key, part):
    own_key = jax.random.fold_in(key, 12)
    shape = (KVH, TOKENS, DH)
    field = jnp.clip(jax.random.normal(own_key, shape, jnp.float32), -4.0, 4.0)
    return field.astype(jnp.bfloat16)


def draw_values(key, part):
    own_key = jax.random.fold_in(key, 13)
    shape = (KVH, TOKENS, DH)
    field = jnp.clip(jax.random.normal(own_key, shape, jnp.float32), -4.0, 4.0)
    return field.astype(jnp.bfloat16)


def draw_out_grad(key, part):
    own_key = jax.random.fold_in(key, 14)
    shape = (KVH, TOKENS, GQ * DH)
    field = jnp.clip(jax.random.normal(own_key, shape, jnp.float32), -4.0, 4.0)
    return field.astype(jnp.bfloat16)


def draw_key_blocks(key, part):
    base = jax.random.fold_in(key, 31)
    count_key, order_key, full_key, giver_key, inner_key = jax.random.split(base, 5)
    shard_total = NBLK // BPS
    counts = jax.random.randint(count_key, (KVH, shard_total, 1), 1, R + 1)
    order = jax.random.randint(order_key, (KVH, shard_total, R), 0, 1 << 20) * R + jnp.arange(R, dtype=jnp.int32)
    below = jnp.sum((order[..., None, :] < order[..., :, None]).astype(jnp.int32), axis=-1)
    is_live = below < counts
    shard = jnp.arange(shard_total, dtype=jnp.int32)[None, :, None]
    offset = jnp.arange(1, R + 1, dtype=jnp.int32)[None, None, :]
    full_row = jax.random.randint(full_key, (KVH, 1, 1), R, shard_total)
    giver = jax.random.randint(giver_key, (KVH, 1, 1), 0, shard_total - R)
    owner = shard - offset
    is_live = (is_live | (shard == full_row) | (owner == giver)) & (owner >= 0)
    inner = jax.random.randint(inner_key, (KVH, shard_total, R), 0, BPS)
    return jnp.where(is_live, owner * BPS + inner, -1).astype(jnp.int32)


def normal_values(stream_key, dims, width, bound, kind=jnp.bfloat16):
    result = width * jax.random.normal(stream_key, dims, jnp.float32)
    return jnp.clip(result, min=-bound, max=bound).astype(kind)


def setup_inputs(seed: int = 0) -> dict:
    key_of = jax.random.split(jax.random.key(seed), 9)
    return {
        "queries": draw_queries(jax.random.fold_in(key_of[8], 71), 0),
        "keys": draw_keys(jax.random.fold_in(key_of[8], 71), 0),
        "values": draw_values(jax.random.fold_in(key_of[8], 71), 0),
        "out_grad": draw_out_grad(jax.random.fold_in(key_of[8], 71), 0),
        "gain_lin": jnp.clip(1.0 + 0.18 * jax.random.normal(key_of[4], (KVH, GQ * DH), jnp.float32), 0.1, 1.9),
        "gain_sparse": jnp.clip(1.0 + 0.18 * jax.random.normal(key_of[5], (KVH, GQ * DH), jnp.float32), 0.1, 1.9),
        "key_blocks": draw_key_blocks(jax.random.fold_in(key_of[8], 71), 0),
        "w_feat": normal_values(key_of[7], (DH, F), DH ** -0.5, 0.5),
    }


norm_epsilon = 1e-06

def feature_map(raw_value):
    return jnp.where(raw_value > 0, raw_value + 1.0, jnp.exp(jnp.minimum(raw_value, 0.0)))

def feature_slope(raw_value):
    return jnp.where(raw_value > 0, 1.0, jnp.exp(jnp.minimum(raw_value, 0.0)))

def norm_backward(value, upstream):
    inverse = lax.rsqrt(lax.optimization_barrier(jnp.mean(value * value, axis=-1, keepdims=True)) + norm_epsilon)
    projected = lax.optimization_barrier(jnp.mean(upstream * value, axis=-1, keepdims=True))
    return inverse * upstream - value * (inverse * inverse * inverse) * projected

def product_rows(left, right):
    return lax.dot_general(left, right, (((1,), (1,)), ((), ())), preferred_element_type=jnp.float32)

def product_cols(left, right):
    return lax.dot_general(left, right, (((0,), (0,)), ((), ())), preferred_element_type=jnp.float32)

def rounded(value):
    return lax.optimization_barrier(value.astype(jnp.bfloat16)).astype(jnp.float32)

def group_grads(queries, keys, values, out_grad, gain_lin, gain_sparse, key_blocks, w_feat):
    highest = lax.Precision.HIGHEST
    scaling = DH ** (-0.5)
    query_rows = queries.reshape(TOKENS * GQ, DH)
    query_raw = jnp.dot(query_rows, w_feat, preferred_element_type=jnp.float32)
    query_feat = feature_map(query_raw).astype(jnp.bfloat16)
    key_raw = jnp.dot(keys, w_feat, preferred_element_type=jnp.float32)
    key_feat = feature_map(key_raw).astype(jnp.bfloat16)
    query_wide = query_feat.reshape(NBLK, BLK, GQ, F).astype(jnp.float32)
    key_wide = key_feat.reshape(NBLK, BLK, F).astype(jnp.float32)
    value_wide = values.reshape(NBLK, BLK, DH).astype(jnp.float32)
    block_total = jnp.einsum('bsf,bsd->bfd', key_wide, value_wide, precision=highest)
    block_state = jnp.concatenate([jnp.zeros((1, F, DH), jnp.float32), jnp.cumsum(block_total, axis=0)[:-1]], axis=0)
    lin_state = jnp.einsum('bthf,bfd->bthd', query_wide, block_state, precision=highest)
    causal = lax.broadcasted_iota(jnp.int32, (BLK, BLK), 0) >= lax.broadcasted_iota(jnp.int32, (BLK, BLK), 1)
    lin_scores = jnp.einsum('bthf,bsf->bhts', query_wide, key_wide, precision=highest)
    lin_weights = rounded(jnp.where(causal, lin_scores, 0.0))
    lin_local = jnp.einsum('bhts,bsd->bthd', lin_weights, value_wide, precision=highest)
    lin_out = (lin_state + lin_local).reshape(TOKENS, GQ, DH)
    upstream = out_grad.reshape(TOKENS, GQ, DH).astype(jnp.float32)
    lin_grad = norm_backward(lin_out, upstream * gain_lin.reshape(GQ, DH))
    key_table = keys.reshape(NBLK, BLK, DH)
    value_table = values.reshape(NBLK, BLK, DH)
    shard_count = NBLK // BPS
    key_count = TOK_DEV + R * BLK
    row_index = lax.broadcasted_iota(jnp.int32, (TOK_DEV, key_count), 0)
    col_index = lax.broadcasted_iota(jnp.int32, (TOK_DEV, key_count), 1)

    def shard_part(shard):
        first_row = (shard * TOK_DEV).astype(jnp.int32)
        query_shard = lax.dynamic_slice_in_dim(queries, first_row, TOK_DEV, 0)
        key_shard = lax.dynamic_slice_in_dim(keys, first_row, TOK_DEV, 0)
        value_shard = lax.dynamic_slice_in_dim(values, first_row, TOK_DEV, 0)
        grad_shard = lax.dynamic_slice_in_dim(out_grad, first_row, TOK_DEV, 0)
        listed = lax.dynamic_index_in_dim(key_blocks, shard, 0, keepdims=False)
        chosen = jnp.maximum(listed, 0).astype(jnp.int32)
        key_all = jnp.concatenate([key_shard, key_table[chosen].reshape(R * BLK, DH)], axis=0)
        value_all = jnp.concatenate([value_shard, value_table[chosen].reshape(R * BLK, DH)], axis=0)
        far_live = jnp.concatenate([jnp.zeros((TOK_DEV,), jnp.bool_), jnp.repeat(listed >= 0, BLK)])
        allowed = (col_index <= row_index) | far_live[None, :]
        key_total = jnp.zeros((key_count, DH), jnp.float32)
        value_total = jnp.zeros((key_count, DH), jnp.float32)
        head_parts = []
        for head_index in range(GQ):
            query_head = query_shard[:, head_index * DH:(head_index + 1) * DH]
            grad_head = grad_shard[:, head_index * DH:(head_index + 1) * DH].astype(jnp.float32)
            gain_head = gain_sparse[head_index * DH:(head_index + 1) * DH]
            logits = jnp.where(allowed, scaling * product_rows(query_head, key_all), -jnp.inf)
            row_max = lax.optimization_barrier(jnp.max(logits, axis=1, keepdims=True))
            exp_terms = jnp.exp(logits - row_max)
            probs = exp_terms / lax.optimization_barrier(jnp.sum(exp_terms, axis=1, keepdims=True))
            probs_half = probs.astype(jnp.bfloat16)
            sparse_out = jnp.dot(probs_half, value_all, preferred_element_type=jnp.float32)
            sparse_grad = norm_backward(sparse_out, grad_head * gain_head).astype(jnp.bfloat16)
            prob_grad = product_rows(sparse_grad, value_all)
            row_inner = lax.optimization_barrier(jnp.sum(sparse_grad.astype(jnp.float32) * sparse_out, axis=1, keepdims=True))
            logit_grad = (scaling * probs * (prob_grad - row_inner)).astype(jnp.bfloat16)
            head_parts.append(jnp.dot(logit_grad, key_all, preferred_element_type=jnp.float32))
            key_total = key_total + product_cols(logit_grad, query_head)
            value_total = value_total + product_cols(probs_half, sparse_grad)
        return (jnp.concatenate(head_parts, axis=1), key_total, value_total)
    query_sparse, key_sparse, value_sparse = lax.map(shard_part, jnp.arange(shard_count, dtype=jnp.int32))
    flat_list = key_blocks.reshape(shard_count * R)
    target = jnp.maximum(flat_list, 0).astype(jnp.int32)
    live_far = (flat_list >= 0)[:, None, None]
    near_keys = key_sparse[:, :TOK_DEV].reshape(NBLK, BLK, DH)
    far_keys = key_sparse[:, TOK_DEV:].reshape(shard_count * R, BLK, DH)
    key_sparse_all = near_keys.at[target].add(jnp.where(live_far, far_keys, 0.0)).reshape(TOKENS, DH)
    near_values = value_sparse[:, :TOK_DEV].reshape(NBLK, BLK, DH)
    far_values = value_sparse[:, TOK_DEV:].reshape(shard_count * R, BLK, DH)
    value_sparse_all = near_values.at[target].add(jnp.where(live_far, far_values, 0.0)).reshape(TOKENS, DH)
    lin_grad_blocks = lin_grad.reshape(NBLK, BLK, GQ, DH)
    lin_half = rounded(lin_grad_blocks)
    state_q_grad = jnp.einsum('bthd,bfd->bthf', lin_grad_blocks, block_state, precision=highest)
    block_cot = jnp.einsum('bthf,bthd->bfd', query_wide, lin_grad_blocks, precision=highest)
    later = jnp.cumsum(block_cot[::-1], axis=0)[::-1]
    carried = jnp.concatenate([later[1:], jnp.zeros((1, F, DH), jnp.float32)], axis=0)
    key_state_grad = jnp.einsum('bsd,bfd->bsf', value_wide, carried, precision=highest)
    value_state_grad = jnp.einsum('bsf,bfd->bsd', key_wide, carried, precision=highest)
    score_grad = rounded(jnp.where(causal, jnp.einsum('bthd,bsd->bhts', lin_half, value_wide, precision=highest), 0.0))
    query_local_grad = jnp.einsum('bhts,bsf->bthf', score_grad, key_wide, precision=highest)
    key_local_grad = jnp.einsum('bhts,bthf->bsf', score_grad, query_wide, precision=highest)
    value_local_grad = jnp.einsum('bhts,bthd->bsd', lin_weights, lin_half, precision=highest)
    raw_q_grad = ((state_q_grad + query_local_grad).reshape(TOKENS * GQ, F) * feature_slope(query_raw)).astype(jnp.bfloat16)
    raw_k_grad = ((key_state_grad + key_local_grad).reshape(TOKENS, F) * feature_slope(key_raw)).astype(jnp.bfloat16)
    query_lin = product_rows(raw_q_grad, w_feat).reshape(TOKENS, GQ * DH)
    key_lin = product_rows(raw_k_grad, w_feat)
    weight_part = product_cols(query_rows, raw_q_grad) + product_cols(keys, raw_k_grad)
    query_grads = (query_sparse.reshape(TOKENS, GQ * DH) + query_lin).astype(jnp.bfloat16)
    key_grads = (key_sparse_all + key_lin).astype(jnp.bfloat16)
    value_grads = (value_sparse_all + (value_state_grad + value_local_grad).reshape(TOKENS, DH)).astype(jnp.bfloat16)
    return (query_grads, key_grads, value_grads, weight_part)

def reference(queries, keys, values, out_grad, gain_lin, gain_sparse, key_blocks, w_feat):

    def per_group(items):
        return group_grads(items[0], items[1], items[2], items[3], items[4], items[5], items[6], w_feat)
    query_grads, key_grads, value_grads, weight_parts = lax.map(per_group, (queries, keys, values, out_grad, gain_lin, gain_sparse, key_blocks))
    w_grad = lax.optimization_barrier(jnp.sum(weight_parts, axis=0)) * (KVH * TOKENS) ** (-0.5)
    return (query_grads, key_grads, value_grads, w_grad)
```

```python
import jax
import jax.numpy as jnp
from jax import lax
from jax.experimental import pallas as pl
from jax.experimental.pallas import tpu as pltpu
from jax.sharding import PartitionSpec as P

INTERPRET = False
EPS = 1e-06
F32 = jnp.float32
BF16 = jnp.bfloat16


def nn(a, b):
    return lax.dot_general(a, b, (((1,), (0,)), ((), ())), preferred_element_type=F32)


def nt(a, b):
    return lax.dot_general(a, b, (((1,), (1,)), ((), ())), preferred_element_type=F32)


def tn(a, b):
    return lax.dot_general(a, b, (((0,), (0,)), ((), ())), preferred_element_type=F32)


def iotas(shape):
    return (
        lax.broadcasted_iota(jnp.int32, shape, 0),
        lax.broadcasted_iota(jnp.int32, shape, 1),
    )


def ones_where(mask):
    return jnp.where(mask, 1.0, 0.0).astype(BF16)


def features(raw):
    low = jnp.exp(jnp.minimum(raw, 0.0))
    up = raw > 0
    return jnp.where(up, raw + 1.0, low), jnp.where(up, 1.0, low)


def norm_backward(value, upstream):
    inverse = lax.rsqrt(jnp.mean(value * value, axis=-1, keepdims=True) + EPS)
    projected = jnp.mean(upstream * value, axis=-1, keepdims=True)
    return inverse * upstream - value * (inverse * inverse * inverse) * projected


def split(value):
    high = value.astype(BF16)
    return high, (value - high.astype(F32)).astype(BF16)


def spread(high, low):
    row, col = iotas((high.shape[0] * 2, high.shape[0]))
    place = row & 7
    piece = 4 * (row >> 3)
    first = ones_where((place < 4) & (col == piece + place))
    second = ones_where((place >= 4) & (col == piece + place - 4))
    return nn(first, high) + nn(second, low)


def tiles(value):
    return value.reshape(value.shape[0] // 8, 8, value.shape[1])


def flat(value):
    return value.reshape(value.shape[0] * 8, value.shape[2])


def send_state_kernel(k_ref, v_ref, w_ref, o_ref):
    keys = k_ref[0]
    values = v_ref[0]
    feat = features(nn(keys, w_ref[...]))[0].astype(BF16)
    total = tn(feat, values).astype(BF16)
    size = 2 * total.shape[0]
    row, col = iotas((size, total.shape[0]))
    place, piece = row & 7, row >> 3
    pick = ones_where((place < 4) & (col == 4 * piece + place))
    row, col = iotas((size, keys.shape[0]))
    place, piece = row & 7, row >> 3
    key_pick = ones_where((place >= 4) & (place < 6) & (col == 2 * piece + place - 4))
    value_pick = ones_where((place >= 6) & (col == 2 * piece + place - 6))
    message = nn(pick, total) + nn(key_pick, keys) + nn(value_pick, values)
    o_ref[...] = tiles(message).astype(BF16)


def delayed(value, by):
    return jnp.concatenate([jnp.zeros_like(value[:by]), value[:-by]], axis=0)


def advanced(value, by):
    return jnp.concatenate([value[by:], jnp.zeros_like(value[:by])], axis=0)


def turned(value, by):
    by = by % 8
    return value if by == 0 else pltpu.roll(value, by, 1)


def prefix_kernel(r_ref, o_ref):
    got = r_ref[...].astype(F32)
    count = got.shape[0]
    place = lax.broadcasted_iota(jnp.int32, got.shape, 1)
    total = jnp.zeros(got.shape[1:], F32)
    parts = []
    for source in range(count):
        parts.append(total)
        total = total + got[source]
    before = jnp.stack(parts)
    both = jnp.where(place < 4, before, turned(before, 4))
    high = both.astype(BF16).astype(F32)
    o_ref[:, 0] = jnp.where(place < 4, high, both - high).astype(BF16)
    turns = [turned(got, by) for by in (0, 2, 4, 6)]
    for slot, first in ((1, 4), (2, 6)):
        out = jnp.zeros_like(got)
        for reach in range(1, 5):
            moved = turns[((2 * (reach - 1) - first) % 8) // 2]
            out = jnp.where(place // 2 == reach - 1, delayed(moved, reach), out)
        o_ref[:, slot] = out.astype(BF16)


def main_kernel(
    q_ref, k_ref, v_ref, g_ref, gl_ref, gs_ref, kb_ref, w_ref, r_ref,
    qo_ref, send_ref, kloc_ref, dk_ref, dv_ref, wq_ref,
):
    shard = lax.axis_index("ctx")
    keys = k_ref[0]
    values = v_ref[0]
    w = w_ref[...]
    length, size = keys.shape
    heads = q_ref.shape[2] // size
    scaling = size ** (-0.5)
    rows = heads * length

    def stacked(ref):
        return jnp.concatenate(
            [ref[0, :, h * size : (h + 1) * size] for h in range(heads)], axis=0
        )

    def gains(ref):
        return jnp.concatenate(
            [
                jnp.broadcast_to(ref[:, h * size : (h + 1) * size], (length, size))
                for h in range(heads)
            ],
            axis=0,
        )

    queries = stacked(q_ref)
    upstream = stacked(g_ref).astype(F32)

    got = r_ref[:, 0].astype(F32)
    states = flat(got).astype(BF16)
    row, col = iotas((states.shape[0] // 2, states.shape[0]))
    where_high = 8 * (row >> 2) + (row & 3)
    state_high = nn(ones_where(col == where_high), states).astype(BF16)
    state_low = nn(ones_where(col == where_high + 4), states).astype(BF16)
    raw = nn(queries, w)
    feat, slope = features(raw)
    feat = feat.astype(BF16)
    key_feat = features(nn(keys, w))[0].astype(BF16)
    row, col = iotas((rows, length))
    causal = (row & (length - 1)) >= col
    weights = jnp.where(causal, nt(feat, key_feat), 0.0).astype(BF16)
    lin_out = nn(feat, state_high) + nn(feat, state_low) + nn(weights, values)
    lin_grad = norm_backward(lin_out, upstream * gains(gl_ref))
    lin_high, lin_low = split(lin_grad)
    score_grad = jnp.where(causal, nt(lin_high, values), 0.0).astype(BF16)
    feat_grad = (
        nt(lin_high, state_high)
        + nt(lin_high, state_low)
        + nt(lin_low, state_high)
        + nn(score_grad, key_feat)
    )
    raw_grad = (feat_grad * slope).astype(BF16)
    query_lin = nt(raw_grad, w)
    cot = tn(feat, lin_high) + tn(feat, lin_low)
    kloc_ref[...] = tn(score_grad, feat)
    value_local = tn(weights, lin_high)
    wq_ref[...] = tn(queries, raw_grad)
    send_ref[:, 0] = tiles(spread(*split(cot))).astype(BF16)

    key_far = flat(r_ref[:, 1].astype(F32)).astype(BF16)
    value_far = flat(r_ref[:, 2].astype(F32)).astype(BF16)
    far = key_far.shape[0]
    listed = kb_ref[0, pl.ds(shard, 1), :]
    place = (lax.broadcasted_iota(jnp.int32, (1, far), 1) & 7) >> 1
    live = jnp.zeros((1, far), F32)
    for reach in range(listed.shape[1]):
        here = jnp.where(listed[:, reach : reach + 1] >= 0, 1.0, 0.0)
        live = jnp.where(place == reach, here, live)
    near_logits = jnp.where(causal, scaling * nt(queries, keys), -jnp.inf)
    far_logits = jnp.where(live > 0.5, scaling * nt(queries, key_far), -jnp.inf)
    top = jnp.maximum(
        jnp.max(near_logits, axis=1, keepdims=True), jnp.max(far_logits, axis=1, keepdims=True)
    )
    near_exp = jnp.exp(near_logits - top)
    far_exp = jnp.exp(far_logits - top)
    norm = 1.0 / (
        jnp.sum(near_exp, axis=1, keepdims=True) + jnp.sum(far_exp, axis=1, keepdims=True)
    )
    near_probs = near_exp * norm
    far_probs = far_exp * norm
    near_half = near_probs.astype(BF16)
    far_half = far_probs.astype(BF16)
    sparse_out = nn(near_half, values) + nn(far_half, value_far)
    sparse_grad = norm_backward(sparse_out, upstream * gains(gs_ref)).astype(BF16)
    inner = jnp.sum(sparse_grad.astype(F32) * sparse_out, axis=1, keepdims=True)
    near_grad = (scaling * near_probs * (nt(sparse_grad, values) - inner)).astype(BF16)
    far_grad = (scaling * far_probs * (nt(sparse_grad, value_far) - inner)).astype(BF16)
    query_out = nn(near_grad, keys) + nn(far_grad, key_far) + query_lin
    for h in range(heads):
        qo_ref[0, :, h * size : (h + 1) * size] = query_out[
            h * length : (h + 1) * length
        ].astype(BF16)
    dk_ref[...] = tn(near_grad, queries)
    dv_ref[...] = tn(near_half, sparse_grad) + value_local
    send_ref[:, 1] = tiles(tn(far_grad, queries)).astype(BF16)
    send_ref[:, 2] = tiles(tn(far_half, sparse_grad)).astype(BF16)


def suffix_kernel(r_ref, o_ref):
    cot = r_ref[:, 0].astype(F32)
    cot = cot + turned(cot, 4)
    count = cot.shape[0]
    place = lax.broadcasted_iota(jnp.int32, cot.shape, 1)
    total = jnp.zeros(cot.shape[1:], F32)
    parts = [None] * count
    for source in range(count - 1, -1, -1):
        parts[source] = total
        total = total + cot[source]
    out = jnp.stack(parts)
    for slot, first in ((1, 4), (2, 6)):
        got = r_ref[:, slot].astype(F32)
        summed = jnp.zeros_like(got)
        for reach in range(1, 5):
            summed = summed + advanced(turned(got, first - 2 * (reach - 1)), reach)
        out = jnp.where((place >= first) & (place < first + 2), summed, out)
    o_ref[...] = out


def key_kernel(
    k_ref, v_ref, w_ref, r_ref, kloc_ref, dk_ref, dv_ref, wq_ref, ko_ref, vo_ref, send_ref
):
    keys = k_ref[0]
    values = v_ref[0]
    w = w_ref[...]
    high, low = split(flat(r_ref[...]))
    count = high.shape[0]
    half, length = count // 2, keys.shape[0]
    row, col = iotas((half, count))
    pick = ones_where(col == 8 * (row >> 2) + (row & 3))
    carried_high = nn(pick, high).astype(BF16)
    carried_low = nn(pick, low).astype(BF16)
    row, col = iotas((length, count))
    at = 8 * (row >> 1) + (row & 1)
    key_pick = ones_where(col == at + 4)
    value_pick = ones_where(col == at + 6)
    key_sum = dk_ref[...] + nn(key_pick, high) + nn(key_pick, low)
    value_sum = dv_ref[...] + nn(value_pick, high) + nn(value_pick, low)
    feat, slope = features(nn(keys, w))
    feat = feat.astype(BF16)
    feat_grad = nt(values, carried_high) + nt(values, carried_low) + kloc_ref[...]
    raw_grad = (feat_grad * slope).astype(BF16)
    ko_ref[0] = (key_sum + nt(raw_grad, w)).astype(BF16)
    vo_ref[0] = (value_sum + nn(feat, carried_high) + nn(feat, carried_low)).astype(BF16)
    weight = wq_ref[...] + tn(keys, raw_grad)
    size = keys.shape[1]
    pair = jnp.concatenate([weight[:, :size], weight[:, size:]], axis=0)
    send_ref[...] = tiles(spread(*split(pair))).astype(BF16)


def gather_sum_kernel(r_ref, o_ref):
    total = jnp.sum(r_ref[...].astype(F32), axis=0)
    total = total + pltpu.roll(total, 4, 0)
    o_ref[...] = jnp.broadcast_to(total[None], o_ref.shape)


def make_scale_kernel(scale):
    def scale_kernel(r_ref, o_ref):
        total = jnp.sum(r_ref[...], axis=0) * scale
        place = lax.broadcasted_iota(jnp.int32, total.shape, 0)
        high = total.astype(BF16).astype(F32)
        tile = jnp.where(place < 4, high, total - high)
        o_ref[...] = jnp.broadcast_to(tile[None], o_ref.shape).astype(BF16)

    return scale_kernel


def weight_kernel(r_ref, o_ref):
    got = flat(r_ref[...].astype(F32)).astype(BF16)
    count = got.shape[0]
    row, col = iotas((count // 2, count))
    at = 8 * (row >> 2) + (row & 3)
    pair = nn(ones_where((col == at) | (col == at + 4)), got)
    length, size = o_ref.shape[0], o_ref.shape[1] // 2
    o_ref[:, :size] = pair[:length]
    o_ref[:, size:] = pair[length:]


def call(kernel, *outs):
    shapes = [jax.ShapeDtypeStruct(shape, dtype) for shape, dtype in outs]
    return pl.pallas_call(
        kernel,
        out_shape=shapes if len(shapes) > 1 else shapes[0],
        interpret=INTERPRET,
    )


def swap(value, axis):
    return lax.all_to_all(value, axis, 0, 0, tiled=False)


def per_device(queries, keys, values, out_grad, gain_lin, gain_sparse, key_blocks, w_feat):
    shards = lax.axis_size("ctx")
    groups = lax.axis_size("heads")
    length, size = keys.shape[1:]
    features_n = w_feat.shape[1]
    scale = (queries.shape[0] * groups * length * shards) ** (-0.5)
    tile = (8, size)
    sent = call(send_state_kernel, ((shards, *tile), BF16))(keys, values, w_feat)
    got = call(prefix_kernel, ((shards, 3, *tile), BF16))(swap(sent, "ctx"))
    query_out, sent, key_local, key_near, value_near, weight_part = call(
        main_kernel,
        (queries.shape, BF16),
        ((shards, 3, *tile), BF16),
        ((length, features_n), F32),
        ((length, size), F32),
        ((length, size), F32),
        ((size, features_n), F32),
    )(
        queries, keys, values, out_grad, gain_lin, gain_sparse, key_blocks, w_feat,
        swap(got, "ctx"),
    )
    got = call(suffix_kernel, ((shards, *tile), F32))(swap(sent, "ctx"))
    key_out, value_out, sent = call(
        key_kernel, (keys.shape, BF16), (values.shape, BF16), ((shards, *tile), BF16)
    )(
        keys, values, w_feat, swap(got, "ctx"), key_local, key_near, value_near, weight_part
    )
    part = call(gather_sum_kernel, ((groups, *tile), F32))(swap(sent, "ctx"))
    part = call(make_scale_kernel(scale), ((shards, *tile), BF16))(swap(part, "heads"))
    weight = call(weight_kernel, (w_feat.shape, F32))(swap(part, "ctx"))
    return query_out, key_out, value_out, weight


def solution(mesh):
    sharded = P("heads", "ctx", None)
    return jax.shard_map(
        per_device,
        mesh=mesh,
        in_specs=(
            sharded,
            sharded,
            sharded,
            sharded,
            P("heads", None),
            P("heads", None),
            P("heads", None, None),
            P(),
        ),
        out_specs=(sharded, sharded, sharded, P()),
        check_vma=False,
    )
```

```python
import jax
import jax.numpy as jnp
from jax import lax
from jax.experimental import pallas as pl
from jax.experimental.pallas import tpu as pltpu
from jax.sharding import PartitionSpec as P

INTERPRET = False
EPS = 1e-06
F32 = jnp.float32
BF16 = jnp.bfloat16


def nn(a, b):
    return lax.dot_general(a, b, (((1,), (0,)), ((), ())), preferred_element_type=F32)


def nt(a, b):
    return lax.dot_general(a, b, (((1,), (1,)), ((), ())), preferred_element_type=F32)


def tn(a, b):
    return lax.dot_general(a, b, (((0,), (0,)), ((), ())), preferred_element_type=F32)


def iotas(shape):
    return (
        lax.broadcasted_iota(jnp.int32, shape, 0),
        lax.broadcasted_iota(jnp.int32, shape, 1),
    )


def ones_where(mask):
    return jnp.where(mask, 1.0, 0.0).astype(BF16)


def features(raw):
    low = jnp.exp(jnp.minimum(raw, 0.0))
    up = raw > 0
    return jnp.where(up, raw + 1.0, low), jnp.where(up, 1.0, low)


def norm_backward(value, upstream):
    inverse = lax.rsqrt(jnp.mean(value * value, axis=-1, keepdims=True) + EPS)
    projected = jnp.mean(upstream * value, axis=-1, keepdims=True)
    return inverse * upstream - value * (inverse * inverse * inverse) * projected


def split(value):
    high = value.astype(BF16)
    return high, (value - high.astype(F32)).astype(BF16)


def spread(high, low):
    row, col = iotas((high.shape[0] * 2, high.shape[0]))
    place = row & 7
    piece = 4 * (row >> 3)
    first = ones_where((place < 4) & (col == piece + place))
    second = ones_where((place >= 4) & (col == piece + place - 4))
    return nn(first, high) + nn(second, low)


def tiles(value):
    return value.reshape(value.shape[0] // 8, 8, value.shape[1])


def flat(value):
    return value.reshape(value.shape[0] * 8, value.shape[2])


def send_state_kernel(k_ref, v_ref, w_ref, o_ref):
    keys = k_ref[0]
    values = v_ref[0]
    feat = features(nn(keys, w_ref[...]))[0].astype(BF16)
    total = tn(feat, values).astype(BF16)
    size = 2 * total.shape[0]
    row, col = iotas((size, total.shape[0]))
    place, piece = row & 7, row >> 3
    pick = ones_where((place < 4) & (col == 4 * piece + place))
    row, col = iotas((size, keys.shape[0]))
    place, piece = row & 7, row >> 3
    key_pick = ones_where((place >= 4) & (place < 6) & (col == 2 * piece + place - 4))
    value_pick = ones_where((place >= 6) & (col == 2 * piece + place - 6))
    message = nn(pick, total) + nn(key_pick, keys) + nn(value_pick, values)
    o_ref[...] = tiles(message).astype(BF16)


def delayed(value, by):
    return jnp.concatenate([jnp.zeros_like(value[:by]), value[:-by]], axis=0)


def advanced(value, by):
    return jnp.concatenate([value[by:], jnp.zeros_like(value[:by])], axis=0)


def turned(value, by):
    by = by % 8
    return value if by == 0 else pltpu.roll(value, by, 1)


def prefix_kernel(r_ref, o_ref):
    got = r_ref[...].astype(F32)
    count = got.shape[0]
    place = lax.broadcasted_iota(jnp.int32, got.shape, 1)
    total = jnp.zeros(got.shape[1:], F32)
    parts = []
    for source in range(count):
        parts.append(total)
        total = total + got[source]
    before = jnp.stack(parts)
    both = jnp.where(place < 4, before, turned(before, 4))
    high = both.astype(BF16).astype(F32)
    o_ref[:, 0] = jnp.where(place < 4, high, both - high).astype(BF16)
    turns = [turned(got, by) for by in (0, 2, 4, 6)]
    for slot, first in ((1, 4), (2, 6)):
        out = jnp.zeros_like(got)
        for reach in range(1, 5):
            moved = turns[((2 * (reach - 1) - first) % 8) // 2]
            out = jnp.where(place // 2 == reach - 1, delayed(moved, reach), out)
        o_ref[:, slot] = out.astype(BF16)


def main_kernel(
    q_ref, k_ref, v_ref, g_ref, gl_ref, gs_ref, kb_ref, w_ref, r_ref,
    qo_ref, send_ref, kloc_ref, dk_ref, dv_ref, wq_ref,
):
    shard = lax.axis_index("ctx")
    keys = k_ref[0]
    values = v_ref[0]
    w = w_ref[...]
    length, size = keys.shape
    heads = q_ref.shape[2] // size
    scaling = size ** (-0.5)
    rows = heads * length

    def stacked(ref):
        return jnp.concatenate(
            [ref[0, :, h * size : (h + 1) * size] for h in range(heads)], axis=0
        )

    def gains(ref):
        return jnp.concatenate(
            [
                jnp.broadcast_to(ref[:, h * size : (h + 1) * size], (length, size))
                for h in range(heads)
            ],
            axis=0,
        )

    queries = stacked(q_ref)
    upstream = stacked(g_ref).astype(F32)

    got = r_ref[:, 0].astype(F32)
    states = flat(got).astype(BF16)
    row, col = iotas((states.shape[0] // 2, states.shape[0]))
    where_high = 8 * (row >> 2) + (row & 3)
    state_high = nn(ones_where(col == where_high), states).astype(BF16)
    state_low = nn(ones_where(col == where_high + 4), states).astype(BF16)
    raw = nn(queries, w)
    feat, slope = features(raw)
    feat = feat.astype(BF16)
    key_feat = features(nn(keys, w))[0].astype(BF16)
    row, col = iotas((rows, length))
    causal = (row & (length - 1)) >= col
    weights = jnp.where(causal, nt(feat, key_feat), 0.0).astype(BF16)
    lin_out = nn(feat, state_high) + nn(feat, state_low) + nn(weights, values)
    lin_grad = norm_backward(lin_out, upstream * gains(gl_ref))
    lin_high, lin_low = split(lin_grad)
    score_grad = jnp.where(causal, nt(lin_high, values), 0.0).astype(BF16)
    feat_grad = (
        nt(lin_high, state_high)
        + nt(lin_high, state_low)
        + nt(lin_low, state_high)
        + nn(score_grad, key_feat)
    )
    raw_grad = (feat_grad * slope).astype(BF16)
    query_lin = nt(raw_grad, w)
    cot = tn(feat, lin_high) + tn(feat, lin_low)
    kloc_ref[...] = tn(score_grad, feat)
    value_local = tn(weights, lin_high)
    wq_ref[...] = tn(queries, raw_grad)
    send_ref[:, 0] = tiles(spread(*split(cot))).astype(BF16)

    key_far = flat(r_ref[:, 1].astype(F32)).astype(BF16)
    value_far = flat(r_ref[:, 2].astype(F32)).astype(BF16)
    far = key_far.shape[0]
    table = kb_ref[0]
    column = lax.broadcasted_iota(jnp.int32, table.shape, 1)
    listed = jnp.max(jnp.where(column == shard, table, -1), axis=1, keepdims=True)
    place = (lax.broadcasted_iota(jnp.int32, (1, far), 1) & 7) >> 1
    live = jnp.zeros((1, far), F32)
    for reach in range(listed.shape[0]):
        here = jnp.where(listed[reach : reach + 1] >= 0, 1.0, 0.0)
        live = jnp.where(place == reach, here, live)
    near_logits = jnp.where(causal, scaling * nt(queries, keys), -jnp.inf)
    far_logits = jnp.where(live > 0.5, scaling * nt(queries, key_far), -jnp.inf)
    top = jnp.maximum(
        jnp.max(near_logits, axis=1, keepdims=True), jnp.max(far_logits, axis=1, keepdims=True)
    )
    near_exp = jnp.exp(near_logits - top)
    far_exp = jnp.exp(far_logits - top)
    norm = 1.0 / (
        jnp.sum(near_exp, axis=1, keepdims=True) + jnp.sum(far_exp, axis=1, keepdims=True)
    )
    near_probs = near_exp * norm
    far_probs = far_exp * norm
    near_half = near_probs.astype(BF16)
    far_half = far_probs.astype(BF16)
    sparse_out = nn(near_half, values) + nn(far_half, value_far)
    sparse_grad = norm_backward(sparse_out, upstream * gains(gs_ref)).astype(BF16)
    inner = jnp.sum(sparse_grad.astype(F32) * sparse_out, axis=1, keepdims=True)
    near_grad = (scaling * near_probs * (nt(sparse_grad, values) - inner)).astype(BF16)
    far_grad = (scaling * far_probs * (nt(sparse_grad, value_far) - inner)).astype(BF16)
    query_out = nn(near_grad, keys) + nn(far_grad, key_far) + query_lin
    for h in range(heads):
        qo_ref[0, :, h * size : (h + 1) * size] = query_out[
            h * length : (h + 1) * length
        ].astype(BF16)
    dk_ref[...] = tn(near_grad, queries)
    dv_ref[...] = tn(near_half, sparse_grad) + value_local
    send_ref[:, 1] = tiles(tn(far_grad, queries)).astype(BF16)
    send_ref[:, 2] = tiles(tn(far_half, sparse_grad)).astype(BF16)


def suffix_kernel(r_ref, o_ref):
    cot = r_ref[:, 0].astype(F32)
    cot = cot + turned(cot, 4)
    count = cot.shape[0]
    place = lax.broadcasted_iota(jnp.int32, cot.shape, 1)
    total = jnp.zeros(cot.shape[1:], F32)
    parts = [None] * count
    for source in range(count - 1, -1, -1):
        parts[source] = total
        total = total + cot[source]
    out = jnp.stack(parts)
    for slot, first in ((1, 4), (2, 6)):
        got = r_ref[:, slot].astype(F32)
        summed = jnp.zeros_like(got)
        for reach in range(1, 5):
            summed = summed + advanced(turned(got, first - 2 * (reach - 1)), reach)
        out = jnp.where((place >= first) & (place < first + 2), summed, out)
    o_ref[...] = out


def key_kernel(
    k_ref, v_ref, w_ref, r_ref, kloc_ref, dk_ref, dv_ref, wq_ref, ko_ref, vo_ref, send_ref
):
    keys = k_ref[0]
    values = v_ref[0]
    w = w_ref[...]
    high, low = split(flat(r_ref[...]))
    count = high.shape[0]
    half, length = count // 2, keys.shape[0]
    row, col = iotas((half, count))
    pick = ones_where(col == 8 * (row >> 2) + (row & 3))
    carried_high = nn(pick, high).astype(BF16)
    carried_low = nn(pick, low).astype(BF16)
    row, col = iotas((length, count))
    at = 8 * (row >> 1) + (row & 1)
    key_pick = ones_where(col == at + 4)
    value_pick = ones_where(col == at + 6)
    key_sum = dk_ref[...] + nn(key_pick, high) + nn(key_pick, low)
    value_sum = dv_ref[...] + nn(value_pick, high) + nn(value_pick, low)
    feat, slope = features(nn(keys, w))
    feat = feat.astype(BF16)
    feat_grad = nt(values, carried_high) + nt(values, carried_low) + kloc_ref[...]
    raw_grad = (feat_grad * slope).astype(BF16)
    ko_ref[0] = (key_sum + nt(raw_grad, w)).astype(BF16)
    vo_ref[0] = (value_sum + nn(feat, carried_high) + nn(feat, carried_low)).astype(BF16)
    weight = wq_ref[...] + tn(keys, raw_grad)
    size = keys.shape[1]
    pair = jnp.concatenate([weight[:, :size], weight[:, size:]], axis=0)
    send_ref[...] = tiles(spread(*split(pair))).astype(BF16)


def gather_sum_kernel(r_ref, o_ref):
    total = jnp.sum(r_ref[...].astype(F32), axis=0)
    total = total + pltpu.roll(total, 4, 0)
    o_ref[...] = jnp.broadcast_to(total[None], o_ref.shape)


def make_scale_kernel(scale):
    def scale_kernel(r_ref, o_ref):
        total = jnp.sum(r_ref[...], axis=0) * scale
        place = lax.broadcasted_iota(jnp.int32, total.shape, 0)
        high = total.astype(BF16).astype(F32)
        tile = jnp.where(place < 4, high, total - high)
        o_ref[...] = jnp.broadcast_to(tile[None], o_ref.shape).astype(BF16)

    return scale_kernel


def weight_kernel(r_ref, o_ref):
    got = flat(r_ref[...].astype(F32)).astype(BF16)
    count = got.shape[0]
    row, col = iotas((count // 2, count))
    at = 8 * (row >> 2) + (row & 3)
    pair = nn(ones_where((col == at) | (col == at + 4)), got)
    length, size = o_ref.shape[0], o_ref.shape[1] // 2
    o_ref[:, :size] = pair[:length]
    o_ref[:, size:] = pair[length:]


def call(kernel, *outs, grant=8):
    shapes = [jax.ShapeDtypeStruct(shape, dtype) for shape, dtype in outs]
    spec = pl.BlockSpec(memory_space=pltpu.VMEM)

    def run(*operands):
        return pl.pallas_call(
            kernel,
            out_shape=shapes if len(shapes) > 1 else shapes[0],
            in_specs=[spec] * len(operands),
            out_specs=[spec] * len(shapes) if len(shapes) > 1 else spec,
            interpret=INTERPRET,
            compiler_params=pltpu.CompilerParams(vmem_limit_bytes=grant << 20),
        )(*operands)

    return run


def swap(value, axis):
    return lax.all_to_all(value, axis, 0, 0, tiled=False)


def per_device(queries, keys, values, out_grad, gain_lin, gain_sparse, key_blocks, w_feat):
    shards = lax.axis_size("ctx")
    groups = lax.axis_size("heads")
    length, size = keys.shape[1:]
    features_n = w_feat.shape[1]
    scale = (queries.shape[0] * groups * length * shards) ** (-0.5)
    tile = (8, size)
    sent = call(send_state_kernel, ((shards, *tile), BF16))(keys, values, w_feat)
    got = call(prefix_kernel, ((shards, 3, *tile), BF16))(swap(sent, "ctx"))
    query_out, sent, key_local, key_near, value_near, weight_part = call(
        main_kernel,
        (queries.shape, BF16),
        ((shards, 3, *tile), BF16),
        ((length, features_n), F32),
        ((length, size), F32),
        ((length, size), F32),
        ((size, features_n), F32),
        grant=24,
    )(
        queries, keys, values, out_grad, gain_lin, gain_sparse,
        jnp.swapaxes(key_blocks, 1, 2), w_feat,
        swap(got, "ctx"),
    )
    got = call(suffix_kernel, ((shards, *tile), F32))(swap(sent, "ctx"))
    key_out, value_out, sent = call(
        key_kernel, (keys.shape, BF16), (values.shape, BF16), ((shards, *tile), BF16)
    )(
        keys, values, w_feat, swap(got, "ctx"), key_local, key_near, value_near, weight_part
    )
    part = call(gather_sum_kernel, ((groups, *tile), F32))(swap(sent, "ctx"))
    part = call(make_scale_kernel(scale), ((shards, *tile), BF16))(swap(part, "heads"))
    weight = call(weight_kernel, (w_feat.shape, F32))(swap(part, "ctx"))
    return query_out, key_out, value_out, weight


def solution(mesh):
    sharded = P("heads", "ctx", None)
    return jax.shard_map(
        per_device,
        mesh=mesh,
        in_specs=(
            sharded,
            sharded,
            sharded,
            sharded,
            P("heads", None),
            P("heads", None),
            P("heads", None, None),
            P(),
        ),
        out_specs=(sharded, sharded, sharded, P()),
        check_vma=False,
    )
```

```python
import jax
import jax.numpy as jnp
from jax import lax
from jax.experimental import pallas as pl
from jax.experimental.pallas import tpu as pltpu
from jax.sharding import PartitionSpec as P

INTERPRET = False
EPS = 1e-06
F32 = jnp.float32
BF16 = jnp.bfloat16


def nn(a, b):
    return lax.dot_general(a, b, (((1,), (0,)), ((), ())), preferred_element_type=F32)


def nt(a, b):
    return lax.dot_general(a, b, (((1,), (1,)), ((), ())), preferred_element_type=F32)


def tn(a, b):
    return lax.dot_general(a, b, (((0,), (0,)), ((), ())), preferred_element_type=F32)


def iotas(shape):
    return (
        lax.broadcasted_iota(jnp.int32, shape, 0),
        lax.broadcasted_iota(jnp.int32, shape, 1),
    )


def ones_where(mask):
    return jnp.where(mask, 1.0, 0.0).astype(BF16)


def features(raw):
    low = jnp.exp(jnp.minimum(raw, 0.0))
    up = raw > 0
    return jnp.where(up, raw + 1.0, low), jnp.where(up, 1.0, low)


def norm_backward(value, upstream):
    inverse = lax.rsqrt(jnp.mean(value * value, axis=-1, keepdims=True) + EPS)
    projected = jnp.mean(upstream * value, axis=-1, keepdims=True)
    return inverse * upstream - value * (inverse * inverse * inverse) * projected


def split(value):
    high = value.astype(BF16)
    return high, (value - high.astype(F32)).astype(BF16)

SIDE = 8


def spots():
    shard = lax.axis_index("ctx")
    return shard // SIDE, shard % SIDE, shard


def flag(condition):
    return jnp.where(condition, 1.0, 0.0).astype(F32)


def pieces(value):
    return value.reshape(SIDE, value.shape[0] // SIDE, value.shape[1])


def whole(value):
    return value.reshape(value.shape[0] * value.shape[1], value.shape[2])


def store_split(ref, at, value):
    step = value.shape[1]
    high, low = split(value)
    ref[:, at : at + step] = high
    ref[:, at + step : at + 2 * step] = low


def send_state_kernel(k_ref, v_ref, w_ref, o_ref):
    keys = k_ref[0]
    values = v_ref[0]
    feat = features(nn(keys, w_ref[...]))[0].astype(BF16)
    total = pieces(tn(feat, values).astype(BF16))
    step, length = total.shape[1], keys.shape[0]
    o_ref[:, :step] = total
    for spot in range(SIDE):
        o_ref[spot, step : step + length] = keys
        o_ref[spot, step + length :] = values


def row_total_kernel(r_ref, o_ref, kv_ref):
    step = o_ref.shape[1]
    total = jnp.sum(r_ref[:, :step].astype(F32), axis=0)
    o_ref[...] = jnp.broadcast_to(total[None], o_ref.shape)
    kv_ref[...] = r_ref[SIDE // 2 :, step:]


def prefix_kernel(r_ref, c_ref, o_ref):
    step = c_ref.shape[1]
    line = spots()[0]
    total = jnp.zeros(c_ref.shape[1:], F32)
    for source in range(SIDE):
        total = total + flag(source < line) * c_ref[source]
    for spot in range(SIDE):
        o_ref[spot, :step], o_ref[spot, step:] = split(total)
        total = total + r_ref[spot, :step].astype(F32)


def main_kernel(
    q_ref, k_ref, v_ref, g_ref, gl_ref, gs_ref, kb_ref, w_ref, row_ref, prev_ref, r_ref,
    qo_ref, send_ref, up_ref, back_ref, kloc_ref, dk_ref, dv_ref,
):
    spot, shard = spots()[1:]
    keys = k_ref[0]
    values = v_ref[0]
    w = w_ref[...]
    length, size = keys.shape
    heads = q_ref.shape[2] // size
    scaling = size ** (-0.5)
    rows = heads * length
    step = r_ref.shape[1] // 2

    def stacked(ref):
        return jnp.concatenate(
            [ref[0, :, h * size : (h + 1) * size] for h in range(heads)], axis=0
        )

    def gains(ref):
        return jnp.concatenate(
            [
                jnp.broadcast_to(ref[:, h * size : (h + 1) * size], (length, size))
                for h in range(heads)
            ],
            axis=0,
        )

    queries = stacked(q_ref)
    upstream = stacked(g_ref).astype(F32)

    state_high = whole(r_ref[:, :step])
    state_low = whole(r_ref[:, step:])
    raw = nn(queries, w)
    feat, slope = features(raw)
    feat = feat.astype(BF16)
    key_feat, key_slope = features(nn(keys, w))
    key_feat = key_feat.astype(BF16)
    row, col = iotas((rows, length))
    causal = (row & (length - 1)) >= col
    weights = jnp.where(causal, nt(feat, key_feat), 0.0).astype(BF16)
    lin_out = nn(feat, state_high) + nn(feat, state_low) + nn(weights, values)
    lin_grad = norm_backward(lin_out, upstream * gains(gl_ref))
    lin_high, lin_low = split(lin_grad)
    score_grad = jnp.where(causal, nt(lin_high, values), 0.0).astype(BF16)
    feat_grad = (
        nt(lin_high, state_high)
        + nt(lin_high, state_low)
        + nt(lin_low, state_high)
        + nn(score_grad, key_feat)
    )
    raw_grad = (feat_grad * slope).astype(BF16)
    query_lin = nt(raw_grad, w)
    key_local = tn(score_grad, feat)
    kloc_ref[...] = key_local
    value_local = tn(weights, lin_high)
    send_ref[:, :step] = pieces(tn(feat, lin_high) + tn(feat, lin_low)).astype(BF16)
    local_high, local_low = split(key_local * key_slope)
    early = tn(raw_grad, queries) + tn(local_high, keys) + tn(local_low, keys)
    store_split(send_ref, step, pieces(early))

    reaches = kb_ref.shape[1]
    table = kb_ref[0]
    column = lax.broadcasted_iota(jnp.int32, table.shape, 1)
    listed = jnp.max(jnp.where(column == shard, table, -1), axis=1, keepdims=True)
    far = []
    live = []
    for reach in range(1, reaches + 1):
        own = row_ref[jnp.maximum(spot - reach, 0), step:].astype(F32)
        other = prev_ref[jnp.clip(spot - reach + SIDE // 2, 0, SIDE // 2 - 1)].astype(F32)
        inside = flag(spot >= reach)
        far.append((inside * own + (1.0 - inside) * other).astype(BF16))
        here = jnp.where(listed[reach - 1 : reach] >= 0, 1.0, 0.0)
        live.append(jnp.broadcast_to(here, (1, length)))
    key_far = jnp.concatenate([item[:length] for item in far], axis=0)
    value_far = jnp.concatenate([item[length:] for item in far], axis=0)
    live = jnp.concatenate(live, axis=1)
    near_logits = jnp.where(causal, scaling * nt(queries, keys), -jnp.inf)
    far_logits = jnp.where(live > 0.5, scaling * nt(queries, key_far), -jnp.inf)
    top = jnp.maximum(
        jnp.max(near_logits, axis=1, keepdims=True), jnp.max(far_logits, axis=1, keepdims=True)
    )
    near_exp = jnp.exp(near_logits - top)
    far_exp = jnp.exp(far_logits - top)
    norm = 1.0 / (
        jnp.sum(near_exp, axis=1, keepdims=True) + jnp.sum(far_exp, axis=1, keepdims=True)
    )
    near_probs = near_exp * norm
    far_probs = far_exp * norm
    near_half = near_probs.astype(BF16)
    far_half = far_probs.astype(BF16)
    sparse_out = nn(near_half, values) + nn(far_half, value_far)
    sparse_grad = norm_backward(sparse_out, upstream * gains(gs_ref)).astype(BF16)
    inner = jnp.sum(sparse_grad.astype(F32) * sparse_out, axis=1, keepdims=True)
    near_grad = (scaling * near_probs * (nt(sparse_grad, values) - inner)).astype(BF16)
    far_grad = (scaling * far_probs * (nt(sparse_grad, value_far) - inner)).astype(BF16)
    query_out = nn(near_grad, keys) + nn(far_grad, key_far) + query_lin
    for h in range(heads):
        qo_ref[0, :, h * size : (h + 1) * size] = query_out[
            h * length : (h + 1) * length
        ].astype(BF16)
    dk_ref[...] = tn(near_grad, queries)
    dv_ref[...] = tn(near_half, sparse_grad) + value_local
    key_back = tn(far_grad, queries).astype(BF16)
    value_back = tn(far_half, sparse_grad).astype(BF16)
    up_ref[...] = jnp.zeros(up_ref.shape, BF16)
    back_ref[...] = jnp.zeros(back_ref.shape, BF16)
    for reach in range(1, reaches + 1):
        part = slice((reach - 1) * length, reach * length)

        @pl.when(spot >= reach)
        def _():
            up_ref[spot - reach, :length] = key_back[part]
            up_ref[spot - reach, length:] = value_back[part]

        @pl.when(spot < reach)
        def _():
            back_ref[spot - reach + SIDE // 2, :length] = key_back[part]
            back_ref[spot - reach + SIDE // 2, length:] = value_back[part]


def cot_total_kernel(r_ref, o_ref):
    step = o_ref.shape[1]
    total = jnp.sum(r_ref[:, :step].astype(F32), axis=0)
    o_ref[...] = jnp.broadcast_to(total[None], o_ref.shape)


def weight_part_kernel(row_ref, w_ref, r_ref, c_ref, send_ref, o_ref):
    line, spot = spots()[:2]
    step, size = c_ref.shape[1:]
    length = (row_ref.shape[1] - step) // 2
    w = w_ref[...]
    row, col = iotas((step, w.shape[1]))
    own = nt(ones_where(col == row + step * spot), w).astype(BF16)
    total = jnp.zeros(c_ref.shape[1:], F32)
    for source in range(SIDE):
        total = total + flag(source > line) * c_ref[source]
    weight = jnp.zeros(c_ref.shape[1:], F32)
    for source in range(SIDE - 1, -1, -1):
        high, low = split(total)
        o_ref[source, :step] = high
        o_ref[source, step:] = low
        keys = row_ref[source, step : step + length]
        values = row_ref[source, step + length :]
        slope = features(nt(own, keys))[1]
        grad_high, grad_low = split((nt(high, values) + nt(low, values)) * slope)
        weight = weight + nn(grad_high, keys) + nn(grad_low, keys)
        for place in (1, 2):
            weight = weight + r_ref[source, place * step : (place + 1) * step].astype(F32)
        total = total + r_ref[source, :step].astype(F32)
    send_ref[...] = jnp.broadcast_to(weight[None], send_ref.shape)


def column_sum_kernel(r_ref, o_ref):
    o_ref[...] = jnp.broadcast_to(jnp.sum(r_ref[...], axis=0)[None], o_ref.shape)


def make_last_kernel(scale):
    def last_kernel(r_ref, carried_ref, up_ref, back_ref, o_ref):
        step = r_ref.shape[1]
        high, low = split(jnp.sum(r_ref[...], axis=0) * scale)
        o_ref[:, : 2 * step] = carried_ref[...]
        o_ref[:, 2 * step : 3 * step] = jnp.broadcast_to(high[None], (SIDE, *high.shape))
        o_ref[:, 3 * step : 4 * step] = jnp.broadcast_to(low[None], (SIDE, *low.shape))
        o_ref[: SIDE // 2, 4 * step :] = up_ref[: SIDE // 2]
        both = up_ref[SIDE // 2 :].astype(F32) + back_ref[...].astype(F32)
        o_ref[SIDE // 2 :, 4 * step :] = both.astype(BF16)

    return last_kernel


def key_kernel(
    k_ref, v_ref, w_ref, r_ref, kloc_ref, dk_ref, dv_ref, ko_ref, vo_ref, wo_ref
):
    keys = k_ref[0]
    values = v_ref[0]
    w = w_ref[...]
    step = w.shape[1] // SIDE
    length = keys.shape[0]
    carried_high = whole(r_ref[:, :step])
    carried_low = whole(r_ref[:, step : 2 * step])
    weight = whole(r_ref[:, 2 * step : 3 * step]).astype(F32)
    weight = weight + whole(r_ref[:, 3 * step : 4 * step]).astype(F32)
    wo_ref[...] = weight.T
    back = jnp.sum(r_ref[:, 4 * step :].astype(F32), axis=0)
    feat, slope = features(nn(keys, w))
    feat = feat.astype(BF16)
    feat_grad = nt(values, carried_high) + nt(values, carried_low) + kloc_ref[...]
    raw_grad = (feat_grad * slope).astype(BF16)
    ko_ref[0] = (dk_ref[...] + back[:length] + nt(raw_grad, w)).astype(BF16)
    vo_ref[0] = (
        dv_ref[...] + back[length:] + nn(feat, carried_high) + nn(feat, carried_low)
    ).astype(BF16)


def call(kernel, *outs, grant=8):
    shapes = [jax.ShapeDtypeStruct(shape, dtype) for shape, dtype in outs]
    spec = pl.BlockSpec(memory_space=pltpu.VMEM)

    def run(*operands):
        return pl.pallas_call(
            kernel,
            out_shape=shapes if len(shapes) > 1 else shapes[0],
            in_specs=[spec] * len(operands),
            out_specs=[spec] * len(shapes) if len(shapes) > 1 else spec,
            interpret=INTERPRET,
            compiler_params=pltpu.CompilerParams(vmem_limit_bytes=grant << 20),
        )(*operands)

    return run


def swap(value, axis, groups=None):
    return lax.all_to_all(value, axis, 0, 0, axis_index_groups=groups, tiled=False)


def per_device(queries, keys, values, out_grad, gain_lin, gain_sparse, key_blocks, w_feat):
    shards = lax.axis_size("ctx")
    groups = lax.axis_size("heads")
    length, size = keys.shape[1:]
    features_n = w_feat.shape[1]
    scale = (queries.shape[0] * groups * length * shards) ** (-0.5)
    step = features_n // SIDE
    in_row = [[line * SIDE + spot for spot in range(SIDE)] for line in range(shards // SIDE)]
    in_column = [[line * SIDE + spot for line in range(shards // SIDE)] for spot in range(SIDE)]
    half = (SIDE // 2, 2 * length, size)
    piece = (SIDE, step, size)
    two = (SIDE, 2 * step, size)
    down = [(i, i + SIDE) for i in range(shards - SIDE)]
    sent = call(send_state_kernel, ((SIDE, step + 2 * length, size), BF16))(keys, values, w_feat)
    row = swap(sent, "ctx", in_row)
    sent, moved = call(row_total_kernel, (piece, F32), (half, BF16))(row)
    previous = lax.ppermute(moved, "ctx", down)
    sent = call(prefix_kernel, (two, BF16))(row, swap(sent, "ctx", in_column))
    query_out, sent, up, back, key_local, key_near, value_near = call(
        main_kernel,
        (queries.shape, BF16),
        ((SIDE, 3 * step, size), BF16),
        ((SIDE, 2 * length, size), BF16),
        (half, BF16),
        ((length, features_n), F32),
        ((length, size), F32),
        ((length, size), F32),
        grant=24,
    )(
        queries, keys, values, out_grad, gain_lin, gain_sparse,
        jnp.swapaxes(key_blocks, 1, 2), w_feat, row, previous, swap(sent, "ctx", in_row),
    )
    returned = lax.ppermute(back, "ctx", [(b, a) for a, b in down])
    cots = swap(sent, "ctx", in_row)
    sent = call(cot_total_kernel, (piece, F32))(cots)
    sent, carried = call(weight_part_kernel, (piece, F32), (two, BF16))(
        row, w_feat, cots, swap(sent, "ctx", in_column)
    )
    sent = call(column_sum_kernel, ((groups, step, size), F32))(swap(sent, "ctx", in_column))
    sent = call(make_last_kernel(scale), ((SIDE, 4 * step + 2 * length, size), BF16))(
        swap(sent, "heads"), carried, up, returned
    )
    key_out, value_out, weight = call(
        key_kernel, (keys.shape, BF16), (values.shape, BF16), (w_feat.shape, F32)
    )(keys, values, w_feat, swap(sent, "ctx", in_row), key_local, key_near, value_near)
    return query_out, key_out, value_out, weight


def solution(mesh):
    sharded = P("heads", "ctx", None)
    return jax.shard_map(
        per_device,
        mesh=mesh,
        in_specs=(
            sharded,
            sharded,
            sharded,
            sharded,
            P("heads", None),
            P("heads", None),
            P("heads", None, None),
            P(),
        ),
        out_specs=(sharded, sharded, sharded, P()),
        check_vma=False,
    )
```

```python
import jax
import jax.numpy as jnp
from jax import lax
from jax.experimental import pallas as pl
from jax.experimental.pallas import tpu as pltpu
from jax.sharding import PartitionSpec as P


INTERPRET = False
EPS = 1e-06
F32 = jnp.float32
BF16 = jnp.bfloat16


def nn(a, b):
    return lax.dot_general(a, b, (((1,), (0,)), ((), ())), preferred_element_type=F32)


def nt(a, b):
    return lax.dot_general(a, b, (((1,), (1,)), ((), ())), preferred_element_type=F32)


def tn(a, b):
    return lax.dot_general(a, b, (((0,), (0,)), ((), ())), preferred_element_type=F32)


def iotas(shape):
    return (
        lax.broadcasted_iota(jnp.int32, shape, 0),
        lax.broadcasted_iota(jnp.int32, shape, 1),
    )


def ones_where(mask):
    return jnp.where(mask, 1.0, 0.0).astype(BF16)


def features(raw):
    low = jnp.exp(jnp.minimum(raw, 0.0))
    up = raw > 0
    return jnp.where(up, raw + 1.0, low), jnp.where(up, 1.0, low)


def norm_backward(value, upstream):
    inverse = lax.rsqrt(jnp.mean(value * value, axis=-1, keepdims=True) + EPS)
    projected = jnp.mean(upstream * value, axis=-1, keepdims=True)
    return inverse * upstream - value * (inverse * inverse * inverse) * projected


def split(value):
    high = value.astype(BF16)
    return high, (value - high.astype(F32)).astype(BF16)


SIDE = 8


def spots():
    shard = lax.axis_index("ctx")
    return shard // SIDE, shard % SIDE, shard


def flag(condition):
    return jnp.where(condition, 1.0, 0.0).astype(F32)


def pieces(value):
    return value.reshape(SIDE, value.shape[0] // SIDE, value.shape[1])


def whole(value):
    return value.reshape(value.shape[0] * value.shape[1], value.shape[2])


def store_split(ref, at, value):
    step = value.shape[1]
    high, low = split(value)
    ref[:, at : at + step] = high
    ref[:, at + step : at + 2 * step] = low


def send_state_kernel(k_hbm, v_hbm, w_hbm, o_ref, k_ref, v_ref, w_ref, sem):
    copies = [
        pltpu.make_async_copy(source, target, sem.at[place])
        for place, (source, target) in enumerate(
            ((k_hbm, k_ref), (v_hbm, v_ref), (w_hbm, w_ref))
        )
    ]
    for copy in copies:
        copy.start()
    for copy in copies:
        copy.wait()
    keys = k_ref[0]
    values = v_ref[0]
    feat = features(nn(keys, w_ref[...]))[0].astype(BF16)
    total = pieces(tn(feat, values).astype(BF16))
    step, length = total.shape[1], keys.shape[0]
    o_ref[:, :step] = total
    for spot in range(SIDE):
        o_ref[spot, step : step + length] = keys
        o_ref[spot, step + length :] = values


def row_total_kernel(r_ref, o_ref, kv_ref):
    step = o_ref.shape[1]
    total = jnp.sum(r_ref[:, :step].astype(F32), axis=0)
    o_ref[...] = jnp.broadcast_to(total[None], o_ref.shape)
    kv_ref[...] = r_ref[SIDE // 2 :, step:]


def prefix_kernel(r_ref, c_ref, o_ref):
    step = c_ref.shape[1]
    line = spots()[0]
    total = jnp.zeros(c_ref.shape[1:], F32)
    for source in range(SIDE):
        total = total + flag(source < line) * c_ref[source]
    for spot in range(SIDE):
        o_ref[spot, :step], o_ref[spot, step:] = split(total)
        total = total + r_ref[spot, :step].astype(F32)


def stacked(ref, size):
    heads = ref.shape[2] // size
    return jnp.concatenate([ref[0, :, h * size : (h + 1) * size] for h in range(heads)], axis=0)


def gains(ref, length, size):
    heads = ref.shape[1] // size
    return jnp.concatenate(
        [
            jnp.broadcast_to(ref[:, h * size : (h + 1) * size], (length, size))
            for h in range(heads)
        ],
        axis=0,
    )


def causal_mask(rows, length):
    row, col = iotas((rows, length))
    return (row & (length - 1)) >= col


def linear_kernel(
    q_ref, k_ref, v_ref, g_ref, gl_ref, w_ref, r_ref, send_ref, kloc_ref, ql_ref, vl_ref
):
    keys = k_ref[0]
    values = v_ref[0]
    w = w_ref[...]
    length, size = keys.shape
    step = r_ref.shape[1] // 2
    queries = stacked(q_ref, size)
    upstream = stacked(g_ref, size).astype(F32)
    state_high = whole(r_ref[:, :step])
    state_low = whole(r_ref[:, step:])
    raw = nn(queries, w)
    feat, slope = features(raw)
    feat = feat.astype(BF16)
    key_feat, key_slope = features(nn(keys, w))
    key_feat = key_feat.astype(BF16)
    causal = causal_mask(queries.shape[0], length)
    weights = jnp.where(causal, nt(feat, key_feat), 0.0).astype(BF16)
    lin_out = nn(feat, state_high) + nn(feat, state_low) + nn(weights, values)
    lin_grad = norm_backward(lin_out, upstream * gains(gl_ref, length, size))
    lin_high, lin_low = split(lin_grad)
    score_grad = jnp.where(causal, nt(lin_high, values), 0.0).astype(BF16)
    feat_grad = (
        nt(lin_high, state_high)
        + nt(lin_high, state_low)
        + nt(lin_low, state_high)
        + nn(score_grad, key_feat)
    )
    raw_grad = (feat_grad * slope).astype(BF16)
    ql_ref[...] = nt(raw_grad, w)
    key_local = tn(score_grad, feat)
    kloc_ref[...] = key_local
    vl_ref[...] = tn(weights, lin_high)
    send_ref[:, :step] = pieces(tn(feat, lin_high) + tn(feat, lin_low)).astype(BF16)
    local_high, local_low = split(key_local * key_slope)
    early = tn(raw_grad, queries) + tn(local_high, keys) + tn(local_low, keys)
    store_split(send_ref, step, pieces(early))


def sparse_kernel(
    q_ref, k_ref, v_ref, g_ref, gs_ref, kb_ref, row_ref, prev_ref, ql_ref, vl_ref,
    qo_ref, dk_ref, dv_ref, *back_refs,
):
    spot, shard = spots()[1:]
    keys = k_ref[0]
    values = v_ref[0]
    length, size = keys.shape
    scaling = size ** (-0.5)
    queries = stacked(q_ref, size)
    heads = queries.shape[0] // length
    upstream = stacked(g_ref, size).astype(F32)
    causal = causal_mask(queries.shape[0], length)
    reaches = kb_ref.shape[1]
    table = kb_ref[0]
    column = lax.broadcasted_iota(jnp.int32, table.shape, 1)
    listed = jnp.max(jnp.where(column == shard, table, -1), axis=1, keepdims=True)
    far = []
    live = []
    for reach in range(1, reaches + 1):
        own = row_ref[jnp.maximum(spot - reach, 0), -2 * length :].astype(F32)
        other = prev_ref[jnp.clip(spot - reach + SIDE // 2, 0, SIDE // 2 - 1)].astype(F32)
        inside = flag(spot >= reach)
        far.append((inside * own + (1.0 - inside) * other).astype(BF16))
        here = jnp.where(listed[reach - 1 : reach] >= 0, 1.0, 0.0)
        live.append(jnp.broadcast_to(here, (1, length)))
    key_far = jnp.concatenate([item[:length] for item in far], axis=0)
    value_far = jnp.concatenate([item[length:] for item in far], axis=0)
    live = jnp.concatenate(live, axis=1)
    near_logits = jnp.where(causal, scaling * nt(queries, keys), -jnp.inf)
    far_logits = jnp.where(live > 0.5, scaling * nt(queries, key_far), -jnp.inf)
    top = jnp.maximum(
        jnp.max(near_logits, axis=1, keepdims=True), jnp.max(far_logits, axis=1, keepdims=True)
    )
    near_exp = jnp.exp(near_logits - top)
    far_exp = jnp.exp(far_logits - top)
    norm = 1.0 / (
        jnp.sum(near_exp, axis=1, keepdims=True) + jnp.sum(far_exp, axis=1, keepdims=True)
    )
    near_probs = near_exp * norm
    far_probs = far_exp * norm
    near_half = near_probs.astype(BF16)
    far_half = far_probs.astype(BF16)
    sparse_out = nn(near_half, values) + nn(far_half, value_far)
    sparse_grad = norm_backward(sparse_out, upstream * gains(gs_ref, length, size)).astype(BF16)
    inner = jnp.sum(sparse_grad.astype(F32) * sparse_out, axis=1, keepdims=True)
    near_grad = (scaling * near_probs * (nt(sparse_grad, values) - inner)).astype(BF16)
    far_grad = (scaling * far_probs * (nt(sparse_grad, value_far) - inner)).astype(BF16)
    query_out = nn(near_grad, keys) + nn(far_grad, key_far) + ql_ref[...]
    for h in range(heads):
        qo_ref[0, :, h * size : (h + 1) * size] = query_out[
            h * length : (h + 1) * length
        ].astype(BF16)
    dk_ref[...] = tn(near_grad, queries)
    dv_ref[...] = tn(near_half, sparse_grad) + vl_ref[...]
    key_back = tn(far_grad, queries).astype(BF16)
    value_back = tn(far_half, sparse_grad).astype(BF16)
    for reach in range(reaches):
        part = slice(reach * length, (reach + 1) * length)
        back_refs[reach][:length] = key_back[part]
        back_refs[reach][length:] = value_back[part]


def total_kernel(r_ref, o_ref):
    step = o_ref.shape[1]
    total = jnp.sum(r_ref[:, :step].astype(F32), axis=0)
    o_ref[...] = jnp.broadcast_to(total[None], o_ref.shape)


def weight_part_kernel(row_ref, w_ref, r_ref, c_ref, a_ref, b_ref, send_ref, o_ref, sum_ref):
    line, spot = spots()[:2]
    step, _ = c_ref.shape[1:]
    length = (row_ref.shape[1] - step) // 2
    w = w_ref[...]
    row, col = iotas((step, w.shape[1]))
    own = nt(ones_where(col == row + step * spot), w).astype(BF16)
    total = jnp.zeros(c_ref.shape[1:], F32)
    for source in range(SIDE):
        total = total + flag(source > line) * c_ref[source]
    weight = jnp.zeros(c_ref.shape[1:], F32)
    for source in range(SIDE - 1, -1, -1):
        high, low = split(total)
        o_ref[source, :step] = high
        o_ref[source, step:] = low
        keys = row_ref[source, step : step + length]
        values = row_ref[source, step + length :]
        slope = features(nt(own, keys))[1]
        grad_high, grad_low = split((nt(high, values) + nt(low, values)) * slope)
        weight = weight + nn(grad_high, keys) + nn(grad_low, keys)
        for place in (1, 2):
            weight = weight + r_ref[source, place * step : (place + 1) * step].astype(F32)
        total = total + r_ref[source, :step].astype(F32)
    send_ref[...] = jnp.broadcast_to(weight[None], send_ref.shape)
    sum_ref[...] = a_ref[...].astype(F32) + b_ref[...].astype(F32)


def column_sum_kernel(r_ref, a_ref, b_ref, in_ref, o_ref, sum_ref):
    sum_ref[...] = in_ref[...] + a_ref[...].astype(F32) + b_ref[...].astype(F32)
    o_ref[...] = jnp.broadcast_to(jnp.sum(r_ref[...], axis=0)[None], o_ref.shape)


def make_last_kernel(scale):
    def last_kernel(r_ref, carried_ref, o_ref):
        step = r_ref.shape[1]
        high, low = split(jnp.sum(r_ref[...], axis=0) * scale)
        o_ref[:, : 2 * step] = carried_ref[...]
        o_ref[:, 2 * step : 3 * step] = jnp.broadcast_to(high[None], (SIDE, *high.shape))
        o_ref[:, 3 * step : 4 * step] = jnp.broadcast_to(low[None], (SIDE, *low.shape))

    return last_kernel


def key_kernel(
    k_ref, v_ref, w_ref, r_ref, kloc_ref, dk_ref, dv_ref, back_ref, ko_ref, vo_ref, wo_ref
):
    keys = k_ref[0]
    values = v_ref[0]
    w = w_ref[...]
    step = w.shape[1] // SIDE
    length = keys.shape[0]
    carried_high = whole(r_ref[:, :step])
    carried_low = whole(r_ref[:, step : 2 * step])
    weight = whole(r_ref[:, 2 * step : 3 * step]).astype(F32)
    weight = weight + whole(r_ref[:, 3 * step : 4 * step]).astype(F32)
    wo_ref[...] = weight.T
    back = back_ref[...]
    feat, slope = features(nn(keys, w))
    feat = feat.astype(BF16)
    feat_grad = nt(values, carried_high) + nt(values, carried_low) + kloc_ref[...]
    raw_grad = (feat_grad * slope).astype(BF16)
    ko_ref[0] = (dk_ref[...] + back[:length] + nt(raw_grad, w)).astype(BF16)
    vo_ref[0] = (
        dv_ref[...] + back[length:] + nn(feat, carried_high) + nn(feat, carried_low)
    ).astype(BF16)


def call(kernel, *outs, grant=8, space=pltpu.VMEM, scratch=()):
    shapes = [jax.ShapeDtypeStruct(shape, dtype) for shape, dtype in outs]
    spec = pl.BlockSpec(memory_space=pltpu.VMEM)

    def run(*operands):
        return pl.pallas_call(
            kernel,
            out_shape=shapes if len(shapes) > 1 else shapes[0],
            in_specs=[pl.BlockSpec(memory_space=space)] * len(operands),
            out_specs=[spec] * len(shapes) if len(shapes) > 1 else spec,
            scratch_shapes=scratch,
            interpret=INTERPRET,
            compiler_params=pltpu.CompilerParams(vmem_limit_bytes=grant << 20),
        )(*operands)

    return run


def swap(value, axis, groups=None):
    return lax.all_to_all(value, axis, 0, 0, axis_index_groups=groups, tiled=False)


def per_device(queries, keys, values, out_grad, gain_lin, gain_sparse, key_blocks, w_feat):
    shards = lax.axis_size("ctx")
    groups = lax.axis_size("heads")
    length, size = keys.shape[1:]
    features_n = w_feat.shape[1]
    scale = (queries.shape[0] * groups * length * shards) ** (-0.5)
    step = features_n // SIDE
    in_row = [[line * SIDE + spot for spot in range(SIDE)] for line in range(shards // SIDE)]
    in_column = [[line * SIDE + spot for line in range(shards // SIDE)] for spot in range(SIDE)]
    half = (SIDE // 2, 2 * length, size)
    piece = (SIDE, step, size)
    two = (SIDE, 2 * step, size)
    down = [(i, i + SIDE) for i in range(shards - SIDE)]
    rows = (queries.shape[2] // size * length, size)
    square = (length, size)
    both = (2 * length, size)
    sent = call(
        send_state_kernel,
        ((SIDE, step + 2 * length, size), BF16),
        space=pltpu.HBM,
        scratch=[pltpu.VMEM(item.shape, BF16) for item in (keys, values, w_feat)]
        + [pltpu.SemaphoreType.DMA((3,))],
    )(keys, values, w_feat)
    row = swap(sent, "ctx", in_row)
    sent, moved = call(row_total_kernel, (piece, F32), (half, BF16))(row)
    got = swap(sent, "ctx", in_column)
    previous = lax.ppermute(moved, "ctx", down)
    sent = call(prefix_kernel, (two, BF16))(row, got)
    got = swap(sent, "ctx", in_row)
    sent, key_local, query_lin, value_local = call(
        linear_kernel,
        ((SIDE, 3 * step, size), BF16),
        ((length, features_n), F32),
        (rows, F32),
        (square, F32),
        grant=16,
    )(queries, keys, values, out_grad, gain_lin, w_feat, got)
    cots = swap(sent, "ctx", in_row)
    query_out, key_near, value_near, *backs = call(
        sparse_kernel,
        (queries.shape, BF16),
        (square, F32),
        (square, F32),
        *[((2 * length, size), BF16)] * key_blocks.shape[2],
        grant=24,
    )(
        queries, keys, values, out_grad, gain_sparse, jnp.swapaxes(key_blocks, 1, 2),
        row, previous, query_lin, value_local,
    )
    far = []
    for reach, back in enumerate(backs, 1):
        pairs = [(i, i - reach) for i in range(reach, shards)]
        far.append(lax.ppermute(back, "ctx", pairs))
    sent = call(total_kernel, (piece, F32))(cots)
    got = swap(sent, "ctx", in_column)
    sent, carried, back = call(
        weight_part_kernel, (piece, F32), (two, BF16), (both, F32)
    )(row, w_feat, cots, got, far[0], far[1])
    got = swap(sent, "ctx", in_column)
    sent, back = call(column_sum_kernel, ((groups, step, size), F32), (both, F32))(
        got, far[2], far[3], back
    )
    got = swap(sent, "heads")
    sent = call(make_last_kernel(scale), ((SIDE, 4 * step, size), BF16))(got, carried)
    got = swap(sent, "ctx", in_row)
    key_out, value_out, weight = call(
        key_kernel, (keys.shape, BF16), (values.shape, BF16), (w_feat.shape, F32)
    )(keys, values, w_feat, got, key_local, key_near, value_near, back)
    return query_out, key_out, value_out, weight


def solution(mesh):
    sharded = P("heads", "ctx", None)
    return jax.shard_map(
        per_device,
        mesh=mesh,
        in_specs=(
            sharded,
            sharded,
            sharded,
            sharded,
            P("heads", None),
            P("heads", None),
            P("heads", None, None),
            P(),
        ),
        out_specs=(sharded, sharded, sharded, P()),
        check_vma=False,
    )
```

```python
import jax
import jax.numpy as jnp
from jax import lax
from jax.experimental import pallas as pl
from jax.experimental.pallas import tpu as pltpu
from jax.sharding import PartitionSpec as P


INTERPRET = False
EPS = 1e-06
F32 = jnp.float32
BF16 = jnp.bfloat16


def nn(a, b):
    return lax.dot_general(a, b, (((1,), (0,)), ((), ())), preferred_element_type=F32)


def nt(a, b):
    return lax.dot_general(a, b, (((1,), (1,)), ((), ())), preferred_element_type=F32)


def tn(a, b):
    return lax.dot_general(a, b, (((0,), (0,)), ((), ())), preferred_element_type=F32)


def iotas(shape):
    return (
        lax.broadcasted_iota(jnp.int32, shape, 0),
        lax.broadcasted_iota(jnp.int32, shape, 1),
    )


def ones_where(mask):
    return jnp.where(mask, 1.0, 0.0).astype(BF16)


def features(raw):
    low = jnp.exp(jnp.minimum(raw, 0.0))
    up = raw > 0
    return jnp.where(up, raw + 1.0, low), jnp.where(up, 1.0, low)


def norm_backward(value, upstream):
    inverse = lax.rsqrt(jnp.mean(value * value, axis=-1, keepdims=True) + EPS)
    projected = jnp.mean(upstream * value, axis=-1, keepdims=True)
    return inverse * upstream - value * (inverse * inverse * inverse) * projected


def split(value):
    high = value.astype(BF16)
    return high, (value - high.astype(F32)).astype(BF16)


SIDE = 8


def spots():
    shard = lax.axis_index("ctx")
    return shard // SIDE, shard % SIDE, shard


def flag(condition):
    return jnp.where(condition, 1.0, 0.0).astype(F32)


def pieces(value):
    return value.reshape(SIDE, value.shape[0] // SIDE, value.shape[1])


def whole(value):
    return value.reshape(value.shape[0] * value.shape[1], value.shape[2])


def send_state_kernel(k_hbm, v_hbm, w_hbm, o_ref, k_ref, v_ref, w_ref, sem):
    copies = [
        pltpu.make_async_copy(source, target, sem.at[place])
        for place, (source, target) in enumerate(
            ((k_hbm, k_ref), (v_hbm, v_ref), (w_hbm, w_ref))
        )
    ]
    for copy in copies:
        copy.start()
    for copy in copies:
        copy.wait()
    keys = k_ref[0]
    values = v_ref[0]
    feat = features(nn(keys, w_ref[...]))[0].astype(BF16)
    total = pieces(tn(feat, values).astype(BF16))
    step, length = total.shape[1], keys.shape[0]
    o_ref[:, :step] = total
    for spot in range(SIDE):
        o_ref[spot, step : step + length] = keys
        o_ref[spot, step + length :] = values


def row_total_kernel(r_ref, o_ref, kv_ref):
    step = o_ref.shape[1]
    total = jnp.sum(r_ref[:, :step].astype(F32), axis=0).astype(BF16)
    for place in range(SIDE):
        o_ref[place] = total
    kv_ref[...] = r_ref[SIDE // 2 :, step:]


def prefix_kernel(r_ref, c_ref, o_ref):
    step = c_ref.shape[1]
    line = spots()[0]
    total = jnp.zeros(c_ref.shape[1:], F32)
    for source in range(SIDE):
        total = total + flag(source < line) * c_ref[source].astype(F32)
    for spot in range(SIDE):
        o_ref[spot] = total.astype(BF16)
        total = total + r_ref[spot, :step].astype(F32)


def stacked(ref, size):
    heads = ref.shape[2] // size
    return jnp.concatenate([ref[0, :, h * size : (h + 1) * size] for h in range(heads)], axis=0)


def gains(ref, length, size):
    heads = ref.shape[1] // size
    return jnp.concatenate(
        [
            jnp.broadcast_to(ref[:, h * size : (h + 1) * size], (length, size))
            for h in range(heads)
        ],
        axis=0,
    )


def causal_mask(rows, length):
    row, col = iotas((rows, length))
    return (row & (length - 1)) >= col


def local_kernel(
    q_ref, k_ref, w_ref, feat_ref, kf_ref, lw_ref,
):
    keys = k_ref[0]
    w = w_ref[...]
    length, size = keys.shape
    queries = stacked(q_ref, size)
    feat = features(nn(queries, w))[0]
    key_feat = features(nn(keys, w))[0]
    causal = causal_mask(queries.shape[0], length)
    scores = nt(feat.astype(BF16), key_feat.astype(BF16))
    feat_ref[...] = feat
    kf_ref[...] = key_feat
    lw_ref[...] = jnp.where(causal, scores, 0.0).astype(BF16)


def linear_kernel(
    q_ref, k_ref, v_ref, g_ref, gl_ref, r_ref, feat_ref, kf_ref, lw_ref,
    send_ref, kloc_ref, rg_ref, lg_ref,
):
    keys = k_ref[0]
    values = v_ref[0]
    length, size = keys.shape
    step = r_ref.shape[1]
    queries = stacked(q_ref, size)
    state = whole(r_ref[...])
    slope = jnp.minimum(feat_ref[...], 1.0)
    key_slope = jnp.minimum(kf_ref[...], 1.0)
    feat = feat_ref[...].astype(BF16)
    key_feat = kf_ref[...].astype(BF16)
    upstream = stacked(g_ref, size).astype(F32)
    lin_out = nn(feat, state) + nn(lw_ref[...], values)
    lin_grad = norm_backward(lin_out, upstream * gains(gl_ref, length, size))
    lin_high, lin_low = split(lin_grad)
    causal = causal_mask(queries.shape[0], length)
    score_grad = jnp.where(causal, nt(lin_high, values), 0.0).astype(BF16)
    feat_grad = nt(lin_high, state) + nt(lin_low, state) + nn(score_grad, key_feat)
    raw_grad = (feat_grad * slope).astype(BF16)
    rg_ref[...] = raw_grad
    lg_ref[...] = lin_high
    key_local = tn(score_grad, feat)
    kloc_ref[...] = key_local
    send_ref[:, :step] = pieces(tn(feat, lin_high) + tn(feat, lin_low)).astype(BF16)
    local_high, local_low = split(key_local * key_slope)
    early = tn(raw_grad, queries) + tn(local_high, keys) + tn(local_low, keys)
    send_ref[:, step:] = pieces(early.astype(BF16))


def sparse_kernel(
    q_ref, k_ref, v_ref, g_ref, gs_ref, kb_ref, row_ref, prev_ref,
    qs_ref, back_ref, dk_ref, dv_ref,
):
    spot, shard = spots()[1:]
    keys = k_ref[0]
    values = v_ref[0]
    length, size = keys.shape
    scaling = size ** (-0.5)
    queries = stacked(q_ref, size)
    upstream = stacked(g_ref, size).astype(F32)
    causal = causal_mask(queries.shape[0], length)
    reaches = kb_ref.shape[1]
    table = kb_ref[0]
    column = lax.broadcasted_iota(jnp.int32, table.shape, 1)
    listed = jnp.max(jnp.where(column == shard, table, -1), axis=1, keepdims=True)
    far = []
    live = []
    for reach in range(1, reaches + 1):
        own = row_ref[jnp.maximum(spot - reach, 0), -2 * length :].astype(F32)
        other = prev_ref[jnp.clip(spot - reach + SIDE // 2, 0, SIDE // 2 - 1)].astype(F32)
        inside = flag(spot >= reach)
        far.append((inside * own + (1.0 - inside) * other).astype(BF16))
        here = jnp.where(listed[reach - 1 : reach] >= 0, 1.0, 0.0)
        live.append(jnp.broadcast_to(here, (1, length)))
    key_far = jnp.concatenate([item[:length] for item in far], axis=0)
    value_far = jnp.concatenate([item[length:] for item in far], axis=0)
    live = jnp.concatenate(live, axis=1)
    near_logits = jnp.where(causal, scaling * nt(queries, keys), -jnp.inf)
    far_logits = jnp.where(live > 0.5, scaling * nt(queries, key_far), -jnp.inf)
    top = jnp.maximum(
        jnp.max(near_logits, axis=1, keepdims=True), jnp.max(far_logits, axis=1, keepdims=True)
    )
    near_exp = jnp.exp(near_logits - top)
    far_exp = jnp.exp(far_logits - top)
    norm = 1.0 / (
        jnp.sum(near_exp, axis=1, keepdims=True) + jnp.sum(far_exp, axis=1, keepdims=True)
    )
    near_probs = near_exp * norm
    far_probs = far_exp * norm
    near_half = near_probs.astype(BF16)
    far_half = far_probs.astype(BF16)
    sparse_out = nn(near_half, values) + nn(far_half, value_far)
    sparse_grad = norm_backward(sparse_out, upstream * gains(gs_ref, length, size)).astype(BF16)
    inner = jnp.sum(sparse_grad.astype(F32) * sparse_out, axis=1, keepdims=True)
    near_grad = (scaling * near_probs * (nt(sparse_grad, values) - inner)).astype(BF16)
    far_grad = (scaling * far_probs * (nt(sparse_grad, value_far) - inner)).astype(BF16)
    qs_ref[...] = nn(near_grad, keys) + nn(far_grad, key_far)
    dk_ref[...] = tn(near_grad, queries)
    dv_ref[...] = tn(near_half, sparse_grad)
    key_back = tn(far_grad, queries).astype(BF16)
    value_back = tn(far_half, sparse_grad).astype(BF16)
    for reach in range(reaches):
        part = slice(reach * length, (reach + 1) * length)
        back_ref[reach, :length] = key_back[part]
        back_ref[reach, length:] = value_back[part]


def finish_kernel(w_ref, rg_ref, lg_ref, lw_ref, qs_ref, dv_ref, qo_ref, vo_ref):
    length, size = dv_ref.shape
    query_out = qs_ref[...] + nt(rg_ref[...], w_ref[...])
    for h in range(qs_ref.shape[0] // length):
        qo_ref[0, :, h * size : (h + 1) * size] = query_out[
            h * length : (h + 1) * length
        ].astype(BF16)
    vo_ref[...] = dv_ref[...] + tn(lw_ref[...], lg_ref[...])


def total_kernel(r_ref, o_ref):
    step = o_ref.shape[1]
    total = jnp.sum(r_ref[:, :step].astype(F32), axis=0).astype(BF16)
    for place in range(SIDE):
        o_ref[place] = total


def slope_kernel(row_ref, w_ref, slope_ref):
    spot = spots()[1]
    w = w_ref[...]
    step, length = slope_ref.shape[1:]
    row, col = iotas((step, w.shape[1]))
    own = nt(ones_where(col == row + step * spot), w).astype(BF16)
    for source in range(SIDE):
        slope_ref[source] = features(nt(own, row_ref[source, step : step + length]))[1]


def weight_part_kernel(
    row_ref, slope_ref, r_ref, c_ref, own_ref, back_ref, send_ref, o_ref, far_ref
):
    line, spot = spots()[:2]
    step, length = slope_ref.shape[1:]
    total = jnp.zeros(c_ref.shape[1:], F32)
    for source in range(SIDE):
        total = total + flag(source > line) * c_ref[source].astype(F32)
    weight = jnp.sum(r_ref[:, step:].astype(F32), axis=0)
    for source in range(SIDE - 1, -1, -1):
        high, low = split(total)
        o_ref[source] = high
        keys = row_ref[source, step : step + length]
        values = row_ref[source, step + length :]
        slope = slope_ref[source]
        grad_high, grad_low = split((nt(high, values) + nt(low, values)) * slope)
        weight = weight + nn(grad_high, keys) + nn(grad_low, keys)
        total = total + r_ref[source, :step].astype(F32)
    weight = weight.astype(BF16)
    for place in range(SIDE):
        send_ref[place] = weight
    far_ref[...] = jnp.zeros(far_ref.shape, BF16)
    for reach in range(1, own_ref.shape[0] + 1):

        @pl.when(spot >= reach)
        def _():
            far_ref[spot - reach] = own_ref[reach - 1]

        @pl.when(spot < reach)
        def _():
            far_ref[spot - reach + SIDE] = back_ref[reach - 1]


def column_sum_kernel(r_ref, o_ref):
    total = jnp.sum(r_ref[...].astype(F32), axis=0).astype(BF16)
    for place in range(o_ref.shape[0]):
        o_ref[place] = total


def make_last_kernel(scale):
    def last_kernel(r_ref, carried_ref, far_ref, o_ref):
        step = r_ref.shape[1]
        high, low = split(jnp.sum(r_ref[...].astype(F32), axis=0) * scale)
        o_ref[:, :step] = carried_ref[...]
        for spot in range(SIDE):
            o_ref[spot, step : 2 * step] = high
            o_ref[spot, 2 * step : 3 * step] = low
        o_ref[:, 3 * step :] = far_ref[...]

    return last_kernel


def key_kernel(
    k_ref, v_ref, w_ref, r_ref, kloc_ref, dk_ref, dv_ref, ko_ref, vo_ref, wo_ref
):
    keys = k_ref[0]
    values = v_ref[0]
    w = w_ref[...]
    step = w.shape[1] // SIDE
    length = keys.shape[0]
    carried = whole(r_ref[:, :step])
    weight = whole(r_ref[:, step : 2 * step]).astype(F32)
    weight = weight + whole(r_ref[:, 2 * step : 3 * step]).astype(F32)
    wo_ref[...] = weight.T
    back = jnp.sum(r_ref[:, 3 * step :].astype(F32), axis=0)
    feat, slope = features(nn(keys, w))
    feat = feat.astype(BF16)
    feat_grad = nt(values, carried) + kloc_ref[...]
    raw_grad = (feat_grad * slope).astype(BF16)
    ko_ref[0] = (dk_ref[...] + back[:length] + nt(raw_grad, w)).astype(BF16)
    vo_ref[0] = (dv_ref[...] + back[length:] + nn(feat, carried)).astype(BF16)


def call(kernel, *outs, grant=8, space=pltpu.VMEM, scratch=()):
    shapes = [jax.ShapeDtypeStruct(shape, dtype) for shape, dtype in outs]
    spec = pl.BlockSpec(memory_space=pltpu.VMEM)

    def run(*operands):
        return pl.pallas_call(
            kernel,
            out_shape=shapes if len(shapes) > 1 else shapes[0],
            in_specs=[pl.BlockSpec(memory_space=space)] * len(operands),
            out_specs=[spec] * len(shapes) if len(shapes) > 1 else spec,
            scratch_shapes=scratch,
            interpret=INTERPRET,
            compiler_params=pltpu.CompilerParams(vmem_limit_bytes=grant << 20),
        )(*operands)

    return run


def swap(value, axis, groups=None):
    return lax.all_to_all(value, axis, 0, 0, axis_index_groups=groups, tiled=False)


def per_device(queries, keys, values, out_grad, gain_lin, gain_sparse, key_blocks, w_feat):
    shards = lax.axis_size("ctx")
    groups = lax.axis_size("heads")
    length, size = keys.shape[1:]
    features_n = w_feat.shape[1]
    scale = (queries.shape[0] * groups * length * shards) ** (-0.5)
    step = features_n // SIDE
    in_row = [[line * SIDE + spot for spot in range(SIDE)] for line in range(shards // SIDE)]
    in_column = [[line * SIDE + spot for line in range(shards // SIDE)] for spot in range(SIDE)]
    half = (SIDE // 2, 2 * length, size)
    piece = (SIDE, step, size)
    down = [(i, i + SIDE) for i in range(shards - SIDE)]
    rows = (queries.shape[2] // size * length, size)
    square = (length, size)
    pair = (SIDE, 2 * length, size)
    sent = call(
        send_state_kernel,
        ((SIDE, step + 2 * length, size), BF16),
        space=pltpu.HBM,
        scratch=[pltpu.VMEM(item.shape, BF16) for item in (keys, values, w_feat)]
        + [pltpu.SemaphoreType.DMA((3,))],
    )(keys, values, w_feat)
    row = swap(sent, "ctx", in_row)
    sent, moved = call(row_total_kernel, (piece, BF16), (half, BF16))(row)
    got = swap(sent, "ctx", in_column)
    previous = lax.ppermute(moved, "ctx", down)
    sent = call(prefix_kernel, (piece, BF16))(row, got)
    got = swap(sent, "ctx", in_row)
    local = call(
        local_kernel,
        ((rows[0], features_n), F32),
        ((length, features_n), F32),
        ((rows[0], length), BF16),
    )(queries, keys, w_feat)
    query_sparse, back, key_near, value_near = call(
        sparse_kernel,
        (rows, F32),
        ((key_blocks.shape[2], 2 * length, size), BF16),
        (square, F32),
        (square, F32),
        grant=12,
    )(
        queries, keys, values, out_grad, gain_sparse, jnp.swapaxes(key_blocks, 1, 2),
        row, previous,
    )
    slopes = call(slope_kernel, ((SIDE, step, length), F32))(row, w_feat)
    sent, key_local, raw_grad, lin_grad = call(
        linear_kernel,
        ((SIDE, 2 * step, size), BF16),
        ((length, features_n), F32),
        ((rows[0], features_n), BF16),
        (rows, BF16),
    )(queries, keys, values, out_grad, gain_lin, got, *local)
    cots = swap(sent, "ctx", in_row)
    returned = lax.ppermute(back, "ctx", [(b, a) for a, b in down])
    query_out, value_near = call(finish_kernel, (queries.shape, BF16), (square, F32))(
        w_feat, raw_grad, lin_grad, local[2], query_sparse, value_near
    )
    sent = call(total_kernel, (piece, BF16))(cots)
    got = swap(sent, "ctx", in_column)
    sent, carried, far = call(
        weight_part_kernel, (piece, BF16), (piece, BF16), (pair, BF16)
    )(row, slopes, cots, got, back, returned)
    got = swap(sent, "ctx", in_column)
    sent = call(column_sum_kernel, ((groups, step, size), BF16))(got)
    got = swap(sent, "heads")
    sent = call(make_last_kernel(scale), ((SIDE, 3 * step + 2 * length, size), BF16))(
        got, carried, far
    )
    got = swap(sent, "ctx", in_row)
    key_out, value_out, weight = call(
        key_kernel, (keys.shape, BF16), (values.shape, BF16), (w_feat.shape, F32)
    )(keys, values, w_feat, got, key_local, key_near, value_near)
    return query_out, key_out, value_out, weight


def solution(mesh):
    sharded = P("heads", "ctx", None)
    return jax.shard_map(
        per_device,
        mesh=mesh,
        in_specs=(
            sharded,
            sharded,
            sharded,
            sharded,
            P("heads", None),
            P("heads", None),
            P("heads", None, None),
            P(),
        ),
        out_specs=(sharded, sharded, sharded, P()),
        check_vma=False,
    )
```

```python
import jax
import jax.numpy as jnp
from jax import lax
from jax.experimental import pallas as pl
from jax.experimental.pallas import tpu as pltpu
from jax.sharding import PartitionSpec as P


INTERPRET = False
EPS = 1e-06
F32 = jnp.float32
BF16 = jnp.bfloat16


def nn(a, b):
    return lax.dot_general(a, b, (((1,), (0,)), ((), ())), preferred_element_type=F32)


def nt(a, b):
    return lax.dot_general(a, b, (((1,), (1,)), ((), ())), preferred_element_type=F32)


def tn(a, b):
    return lax.dot_general(a, b, (((0,), (0,)), ((), ())), preferred_element_type=F32)


def iotas(shape):
    return (
        lax.broadcasted_iota(jnp.int32, shape, 0),
        lax.broadcasted_iota(jnp.int32, shape, 1),
    )


def ones_where(mask):
    return jnp.where(mask, 1.0, 0.0).astype(BF16)


def features(raw):
    low = jnp.exp(jnp.minimum(raw, 0.0))
    up = raw > 0
    return jnp.where(up, raw + 1.0, low), jnp.where(up, 1.0, low)


def norm_backward(value, upstream):
    inverse = lax.rsqrt(jnp.mean(value * value, axis=-1, keepdims=True) + EPS)
    projected = jnp.mean(upstream * value, axis=-1, keepdims=True)
    return inverse * upstream - value * (inverse * inverse * inverse) * projected


def split(value):
    high = value.astype(BF16)
    return high, (value - high.astype(F32)).astype(BF16)


SIDE = 8


def spots():
    shard = lax.axis_index("ctx")
    return shard // SIDE, shard % SIDE, shard


def flag(condition):
    return jnp.where(condition, 1.0, 0.0).astype(F32)


def pieces(value):
    return value.reshape(SIDE, value.shape[0] // SIDE, value.shape[1])


def whole(value):
    return value.reshape(value.shape[0] * value.shape[1], value.shape[2])


def send_state_kernel(k_hbm, v_hbm, w_hbm, o_ref, k_ref, v_ref, w_ref, sem):
    copies = [
        pltpu.make_async_copy(source, target, sem.at[place])
        for place, (source, target) in enumerate(
            ((k_hbm, k_ref), (v_hbm, v_ref), (w_hbm, w_ref))
        )
    ]
    for copy in copies:
        copy.start()
    for copy in copies:
        copy.wait()
    keys = k_ref[0]
    values = v_ref[0]
    feat = features(nn(keys, w_ref[...]))[0].astype(BF16)
    total = pieces(tn(feat, values).astype(BF16))
    step, length = total.shape[1], keys.shape[0]
    o_ref[:, :step] = total
    for spot in range(SIDE):
        o_ref[spot, step : step + length] = keys
        o_ref[spot, step + length :] = values


def row_total_kernel(r_ref, o_ref, kv_ref):
    step = o_ref.shape[1]
    total = jnp.sum(r_ref[:, :step].astype(F32), axis=0).astype(BF16)
    for place in range(SIDE):
        o_ref[place] = total
    kv_ref[...] = r_ref[SIDE // 2 :, step:]


def prefix_kernel(r_ref, c_ref, o_ref):
    step = c_ref.shape[1]
    line = spots()[0]
    total = jnp.zeros(c_ref.shape[1:], F32)
    for source in range(SIDE):
        total = total + flag(source < line) * c_ref[source].astype(F32)
    for spot in range(SIDE):
        o_ref[spot] = total.astype(BF16)
        total = total + r_ref[spot, :step].astype(F32)


def stacked(ref, size):
    heads = ref.shape[2] // size
    return jnp.concatenate([ref[0, :, h * size : (h + 1) * size] for h in range(heads)], axis=0)


def gains(ref, length, size):
    heads = ref.shape[1] // size
    return jnp.concatenate(
        [
            jnp.broadcast_to(ref[:, h * size : (h + 1) * size], (length, size))
            for h in range(heads)
        ],
        axis=0,
    )


def causal_mask(rows, length):
    row, col = iotas((rows, length))
    return (row & (length - 1)) >= col


def local_kernel(
    q_ref, k_ref, w_ref, gl_ref, feat_ref, kf_ref, lw_ref, gain_ref,
):
    keys = k_ref[0]
    w = w_ref[...]
    length, size = keys.shape
    queries = stacked(q_ref, size)
    feat = features(nn(queries, w))[0]
    key_feat = features(nn(keys, w))[0]
    causal = causal_mask(queries.shape[0], length)
    scores = nt(feat.astype(BF16), key_feat.astype(BF16))
    feat_ref[...] = feat
    kf_ref[...] = key_feat
    lw_ref[...] = jnp.where(causal, scores, 0.0).astype(BF16)
    gain_ref[...] = gl_ref[...]


def linear_kernel(
    q_ref, k_ref, v_ref, g_ref, r_ref, feat_ref, kf_ref, lw_ref, gl_ref,
    send_ref, kloc_ref, rg_ref, lg_ref,
):
    keys = k_ref[0]
    values = v_ref[0]
    length, size = keys.shape
    step = r_ref.shape[1]
    queries = stacked(q_ref, size)
    state = whole(r_ref[...])
    slope = jnp.minimum(feat_ref[...], 1.0)
    key_slope = jnp.minimum(kf_ref[...], 1.0)
    feat = feat_ref[...].astype(BF16)
    key_feat = kf_ref[...].astype(BF16)
    upstream = stacked(g_ref, size).astype(F32)
    lin_out = nn(feat, state) + nn(lw_ref[...], values)
    lin_grad = norm_backward(lin_out, upstream * gains(gl_ref, length, size))
    lin_high, lin_low = split(lin_grad)
    causal = causal_mask(queries.shape[0], length)
    score_grad = jnp.where(causal, nt(lin_high, values), 0.0).astype(BF16)
    feat_grad = nt(lin_high, state) + nt(lin_low, state) + nn(score_grad, key_feat)
    raw_grad = (feat_grad * slope).astype(BF16)
    rg_ref[...] = raw_grad
    lg_ref[...] = lin_high
    key_local = tn(score_grad, feat)
    kloc_ref[...] = key_local
    send_ref[:, :step] = pieces(tn(feat, lin_high) + tn(feat, lin_low)).astype(BF16)
    local_high, local_low = split(key_local * key_slope)
    early = tn(raw_grad, queries) + tn(local_high, keys) + tn(local_low, keys)
    send_ref[:, step:] = pieces(early.astype(BF16))


def sparse_kernel(
    q_ref, k_ref, v_ref, g_ref, gs_ref, kb_ref, row_ref, prev_ref,
    qs_ref, back_ref, dk_ref, dv_ref,
):
    spot, shard = spots()[1:]
    keys = k_ref[0]
    values = v_ref[0]
    length, size = keys.shape
    scaling = size ** (-0.5)
    queries = stacked(q_ref, size)
    upstream = stacked(g_ref, size).astype(F32)
    causal = causal_mask(queries.shape[0], length)
    reaches = kb_ref.shape[1]
    table = kb_ref[0]
    column = lax.broadcasted_iota(jnp.int32, table.shape, 1)
    listed = jnp.max(jnp.where(column == shard, table, -1), axis=1, keepdims=True)
    far = []
    live = []
    for reach in range(1, reaches + 1):
        own = row_ref[jnp.maximum(spot - reach, 0), -2 * length :].astype(F32)
        other = prev_ref[jnp.clip(spot - reach + SIDE // 2, 0, SIDE // 2 - 1)].astype(F32)
        inside = flag(spot >= reach)
        far.append((inside * own + (1.0 - inside) * other).astype(BF16))
        here = jnp.where(listed[reach - 1 : reach] >= 0, 1.0, 0.0)
        live.append(jnp.broadcast_to(here, (1, length)))
    key_far = jnp.concatenate([item[:length] for item in far], axis=0)
    value_far = jnp.concatenate([item[length:] for item in far], axis=0)
    live = jnp.concatenate(live, axis=1)
    near_logits = jnp.where(causal, scaling * nt(queries, keys), -jnp.inf)
    far_logits = jnp.where(live > 0.5, scaling * nt(queries, key_far), -jnp.inf)
    top = jnp.maximum(
        jnp.max(near_logits, axis=1, keepdims=True), jnp.max(far_logits, axis=1, keepdims=True)
    )
    near_exp = jnp.exp(near_logits - top)
    far_exp = jnp.exp(far_logits - top)
    norm = 1.0 / (
        jnp.sum(near_exp, axis=1, keepdims=True) + jnp.sum(far_exp, axis=1, keepdims=True)
    )
    near_probs = near_exp * norm
    far_probs = far_exp * norm
    near_half = near_probs.astype(BF16)
    far_half = far_probs.astype(BF16)
    sparse_out = nn(near_half, values) + nn(far_half, value_far)
    sparse_grad = norm_backward(sparse_out, upstream * gains(gs_ref, length, size)).astype(BF16)
    inner = jnp.sum(sparse_grad.astype(F32) * sparse_out, axis=1, keepdims=True)
    near_grad = (scaling * near_probs * (nt(sparse_grad, values) - inner)).astype(BF16)
    far_grad = (scaling * far_probs * (nt(sparse_grad, value_far) - inner)).astype(BF16)
    qs_ref[...] = nn(near_grad, keys) + nn(far_grad, key_far)
    dk_ref[...] = tn(near_grad, queries)
    dv_ref[...] = tn(near_half, sparse_grad)
    key_back = tn(far_grad, queries).astype(BF16)
    value_back = tn(far_half, sparse_grad).astype(BF16)
    for reach in range(reaches):
        part = slice(reach * length, (reach + 1) * length)
        back_ref[reach, :length] = key_back[part]
        back_ref[reach, length:] = value_back[part]


def finish_kernel(w_ref, rg_ref, lg_ref, lw_ref, qs_ref, dv_ref, qo_ref, vo_ref):
    length, size = dv_ref.shape
    query_out = qs_ref[...] + nt(rg_ref[...], w_ref[...])
    for h in range(qs_ref.shape[0] // length):
        qo_ref[0, :, h * size : (h + 1) * size] = query_out[
            h * length : (h + 1) * length
        ].astype(BF16)
    vo_ref[...] = dv_ref[...] + tn(lw_ref[...], lg_ref[...])


def total_kernel(r_ref, o_ref):
    step = o_ref.shape[1]
    total = jnp.sum(r_ref[:, :step].astype(F32), axis=0).astype(BF16)
    for place in range(SIDE):
        o_ref[place] = total


def slope_kernel(row_ref, w_ref, slope_ref):
    spot = spots()[1]
    w = w_ref[...]
    step, length = slope_ref.shape[1:]
    row, col = iotas((step, w.shape[1]))
    own = nt(ones_where(col == row + step * spot), w).astype(BF16)
    for source in range(SIDE):
        slope_ref[source] = features(nt(own, row_ref[source, step : step + length]))[1]


def weight_part_kernel(
    row_ref, slope_ref, r_ref, c_ref, own_ref, back_ref,
    send_ref, o_ref, keep_ref, give_ref,
):
    line, spot = spots()[:2]
    step, length = slope_ref.shape[1:]
    total = jnp.zeros(c_ref.shape[1:], F32)
    for source in range(SIDE):
        total = total + flag(source > line) * c_ref[source].astype(F32)
    weight = jnp.sum(r_ref[:, step:].astype(F32), axis=0)
    for source in range(SIDE - 1, -1, -1):
        high, low = split(total)
        o_ref[source] = high
        keys = row_ref[source, step : step + length]
        values = row_ref[source, step + length :]
        slope = slope_ref[source]
        grad_high, grad_low = split((nt(high, values) + nt(low, values)) * slope)
        weight = weight + nn(grad_high, keys) + nn(grad_low, keys)
        total = total + r_ref[source, :step].astype(F32)
    weight = weight.astype(BF16)
    for place in range(SIDE):
        send_ref[place] = weight
    keep_ref[...] = jnp.zeros(keep_ref.shape, BF16)
    give_ref[...] = jnp.zeros(give_ref.shape, BF16)
    for parity, own, other in ((0, keep_ref, give_ref), (1, give_ref, keep_ref)):
        for reach in range(1, own_ref.shape[0] + 1):

            @pl.when((spot % 2 == parity) & (spot >= reach))
            def _():
                own[spot - reach] = own_ref[reach - 1, :length]
                other[spot - reach] = own_ref[reach - 1, length:]

            @pl.when((spot % 2 == parity) & (spot < reach))
            def _():
                own[spot - reach + SIDE] = back_ref[reach - 1, :length]
                other[spot - reach + SIDE] = back_ref[reach - 1, length:]


def column_sum_kernel(r_ref, o_ref):
    total = jnp.sum(r_ref[...].astype(F32), axis=0).astype(BF16)
    for place in range(o_ref.shape[0]):
        o_ref[place] = total


def make_last_kernel(scale):
    def last_kernel(r_ref, carried_ref, keep_ref, got_ref, o_ref):
        step = r_ref.shape[1]
        high, low = split(jnp.sum(r_ref[...].astype(F32), axis=0) * scale)
        o_ref[:, :step] = carried_ref[...]
        for spot in range(SIDE):
            o_ref[spot, step : 2 * step] = high
            o_ref[spot, 2 * step : 3 * step] = low
        for spot in range(SIDE):
            far = keep_ref[spot].astype(F32) + got_ref[spot].astype(F32)
            o_ref[spot, 3 * step :] = far.astype(BF16)

    return last_kernel


def key_kernel(
    k_ref, v_ref, w_ref, r_ref, kloc_ref, dk_ref, dv_ref, ko_ref, vo_ref, wo_ref
):
    keys = k_ref[0]
    values = v_ref[0]
    w = w_ref[...]
    step = w.shape[1] // SIDE
    carried = whole(r_ref[:, :step])
    weight = whole(r_ref[:, step : 2 * step]).astype(F32)
    weight = weight + whole(r_ref[:, 2 * step : 3 * step]).astype(F32)
    wo_ref[...] = weight.T
    key_back, value_back = (
        sum(r_ref[spot, 3 * step :].astype(F32) for spot in range(parity, SIDE, 2))
        for parity in range(2)
    )
    feat, slope = features(nn(keys, w))
    feat = feat.astype(BF16)
    feat_grad = nt(values, carried) + kloc_ref[...]
    raw_grad = (feat_grad * slope).astype(BF16)
    ko_ref[0] = (dk_ref[...] + key_back + nt(raw_grad, w)).astype(BF16)
    vo_ref[0] = (dv_ref[...] + value_back + nn(feat, carried)).astype(BF16)


def call(kernel, *outs, grant=8, space=pltpu.VMEM, scratch=()):
    shapes = [jax.ShapeDtypeStruct(shape, dtype) for shape, dtype in outs]
    spec = pl.BlockSpec(memory_space=pltpu.VMEM)

    def run(*operands):
        return pl.pallas_call(
            kernel,
            out_shape=shapes if len(shapes) > 1 else shapes[0],
            in_specs=[pl.BlockSpec(memory_space=space)] * len(operands),
            out_specs=[spec] * len(shapes) if len(shapes) > 1 else spec,
            scratch_shapes=scratch,
            interpret=INTERPRET,
            compiler_params=pltpu.CompilerParams(vmem_limit_bytes=grant << 20),
        )(*operands)

    return run


def swap(value, axis, groups=None):
    return lax.all_to_all(value, axis, 0, 0, axis_index_groups=groups, tiled=False)


def per_device(queries, keys, values, out_grad, gain_lin, gain_sparse, key_blocks, w_feat):
    shards = lax.axis_size("ctx")
    groups = lax.axis_size("heads")
    length, size = keys.shape[1:]
    features_n = w_feat.shape[1]
    scale = (queries.shape[0] * groups * length * shards) ** (-0.5)
    step = features_n // SIDE
    in_row = [[line * SIDE + spot for spot in range(SIDE)] for line in range(shards // SIDE)]
    in_column = [[line * SIDE + spot for line in range(shards // SIDE)] for spot in range(SIDE)]
    half = (SIDE // 2, 2 * length, size)
    piece = (SIDE, step, size)
    down = [(i, i + SIDE) for i in range(shards - SIDE)]
    rows = (queries.shape[2] // size * length, size)
    square = (length, size)
    single = (SIDE, length, size)
    sent = call(
        send_state_kernel,
        ((SIDE, step + 2 * length, size), BF16),
        space=pltpu.HBM,
        scratch=[pltpu.VMEM(item.shape, BF16) for item in (keys, values, w_feat)]
        + [pltpu.SemaphoreType.DMA((3,))],
    )(keys, values, w_feat)
    row = swap(sent, "ctx", in_row)
    sent, moved = call(row_total_kernel, (piece, BF16), (half, BF16))(row)
    got = swap(sent, "ctx", in_column)
    previous = lax.ppermute(moved, "ctx", down)
    sent = call(prefix_kernel, (piece, BF16))(row, got)
    got = swap(sent, "ctx", in_row)
    local = call(
        local_kernel,
        ((rows[0], features_n), F32),
        ((length, features_n), F32),
        ((rows[0], length), BF16),
        (gain_lin.shape, F32),
    )(queries, keys, w_feat, gain_lin)
    query_sparse, back, key_near, value_near = call(
        sparse_kernel,
        (rows, F32),
        ((key_blocks.shape[2], 2 * length, size), BF16),
        (square, F32),
        (square, F32),
        grant=12,
    )(
        queries, keys, values, out_grad, gain_sparse, jnp.swapaxes(key_blocks, 1, 2),
        row, previous,
    )
    slopes = call(slope_kernel, ((SIDE, step, length), F32))(row, w_feat)
    sent, key_local, raw_grad, lin_grad = call(
        linear_kernel,
        ((SIDE, 2 * step, size), BF16),
        ((length, features_n), F32),
        ((rows[0], features_n), BF16),
        (rows, BF16),
    )(queries, keys, values, out_grad, got, *local)
    cots = swap(sent, "ctx", in_row)
    returned = lax.ppermute(back, "ctx", [(b, a) for a, b in down])
    query_out, value_near = call(finish_kernel, (queries.shape, BF16), (square, F32))(
        w_feat, raw_grad, lin_grad, local[2], query_sparse, value_near
    )
    sent = call(total_kernel, (piece, BF16))(cots)
    got = swap(sent, "ctx", in_column)
    sent, carried, keep, give = call(
        weight_part_kernel, (piece, BF16), (piece, BF16), (single, BF16), (single, BF16)
    )(row, slopes, cots, got, back, returned)
    taken = lax.ppermute(give, "ctx", [(i, i ^ 1) for i in range(shards)])
    got = swap(sent, "ctx", in_column)
    sent = call(column_sum_kernel, ((groups, step, size), BF16))(got)
    got = swap(sent, "heads")
    sent = call(make_last_kernel(scale), ((SIDE, 3 * step + length, size), BF16))(
        got, carried, keep, taken
    )
    got = swap(sent, "ctx", in_row)
    key_out, value_out, weight = call(
        key_kernel, (keys.shape, BF16), (values.shape, BF16), (w_feat.shape, F32)
    )(keys, values, w_feat, got, key_local, key_near, value_near)
    return query_out, key_out, value_out, weight


def solution(mesh):
    sharded = P("heads", "ctx", None)
    return jax.shard_map(
        per_device,
        mesh=mesh,
        in_specs=(
            sharded,
            sharded,
            sharded,
            sharded,
            P("heads", None),
            P("heads", None),
            P("heads", None, None),
            P(),
        ),
        out_specs=(sharded, sharded, sharded, P()),
        check_vma=False,
    )
```

```python
import jax
import jax.numpy as jnp
from jax import lax
from jax.experimental import pallas as pl
from jax.experimental.pallas import tpu as pltpu
from jax.sharding import PartitionSpec as P


INTERPRET = False
EPS = 1e-06
F32 = jnp.float32
BF16 = jnp.bfloat16


def nn(a, b):
    return lax.dot_general(a, b, (((1,), (0,)), ((), ())), preferred_element_type=F32)


def nt(a, b):
    return lax.dot_general(a, b, (((1,), (1,)), ((), ())), preferred_element_type=F32)


def tn(a, b):
    return lax.dot_general(a, b, (((0,), (0,)), ((), ())), preferred_element_type=F32)


def iotas(shape):
    return (
        lax.broadcasted_iota(jnp.int32, shape, 0),
        lax.broadcasted_iota(jnp.int32, shape, 1),
    )


def ones_where(mask):
    return jnp.where(mask, 1.0, 0.0).astype(BF16)


def features(raw):
    low = jnp.exp(jnp.minimum(raw, 0.0))
    up = raw > 0
    return jnp.where(up, raw + 1.0, low), jnp.where(up, 1.0, low)


def norm_backward(value, upstream):
    inverse = lax.rsqrt(jnp.mean(value * value, axis=-1, keepdims=True) + EPS)
    projected = jnp.mean(upstream * value, axis=-1, keepdims=True)
    return inverse * upstream - value * (inverse * inverse * inverse) * projected


def split(value):
    high = value.astype(BF16)
    return high, (value - high.astype(F32)).astype(BF16)


SIDE = 8


def spots():
    shard = lax.axis_index("ctx")
    return shard // SIDE, shard % SIDE, shard


def flag(condition):
    return jnp.where(condition, 1.0, 0.0).astype(F32)


def pieces(value):
    return value.reshape(SIDE, value.shape[0] // SIDE, value.shape[1])


def whole(value):
    return value.reshape(value.shape[0] * value.shape[1], value.shape[2])


def send_state_kernel(k_hbm, v_hbm, w_hbm, o_ref, k_ref, v_ref, w_ref, sem):
    copies = [
        pltpu.make_async_copy(source, target, sem.at[place])
        for place, (source, target) in enumerate(
            ((k_hbm, k_ref), (v_hbm, v_ref), (w_hbm, w_ref))
        )
    ]
    for copy in copies:
        copy.start()
    for copy in copies:
        copy.wait()
    keys = k_ref[0]
    values = v_ref[0]
    feat = features(nn(keys, w_ref[...]))[0].astype(BF16)
    total = pieces(tn(feat, values).astype(BF16))
    step = total.shape[1]
    o_ref[:, :step] = total
    for spot in range(SIDE):
        o_ref[spot, step:] = values if spot % 2 else keys


def row_total_kernel(r_ref, o_ref, half_ref, moved_ref):
    step = o_ref.shape[1]
    total = jnp.sum(r_ref[:, :step].astype(F32), axis=0).astype(BF16)
    for place in range(SIDE):
        o_ref[place] = total
    half_ref[...] = r_ref[:, step:]
    moved_ref[...] = r_ref[SIDE // 2 :, step:]


def pack_kernel(a_ref, b_ref, o_ref):
    o_ref[:SIDE] = a_ref[...]
    o_ref[SIDE:] = b_ref[...]


def prefix_kernel(r_ref, c_ref, o_ref):
    step = c_ref.shape[1]
    line = spots()[0]
    total = jnp.zeros(c_ref.shape[1:], F32)
    for source in range(SIDE):
        total = total + flag(source < line) * c_ref[source].astype(F32)
    for spot in range(SIDE):
        o_ref[spot] = total.astype(BF16)
        total = total + r_ref[spot, :step].astype(F32)


def stacked(ref, size):
    heads = ref.shape[2] // size
    return jnp.concatenate([ref[0, :, h * size : (h + 1) * size] for h in range(heads)], axis=0)


def gains(ref, length, size):
    heads = ref.shape[1] // size
    return jnp.concatenate(
        [
            jnp.broadcast_to(ref[:, h * size : (h + 1) * size], (length, size))
            for h in range(heads)
        ],
        axis=0,
    )


def causal_mask(rows, length):
    row, col = iotas((rows, length))
    return (row & (length - 1)) >= col


def local_kernel(
    q_ref, k_ref, w_ref, gl_ref, gs_ref, kb_ref,
    feat_ref, kf_ref, lw_ref, gain_ref, sparse_gain_ref, table_ref,
):
    keys = k_ref[0]
    w = w_ref[...]
    length, size = keys.shape
    queries = stacked(q_ref, size)
    feat = features(nn(queries, w))[0]
    key_feat = features(nn(keys, w))[0]
    causal = causal_mask(queries.shape[0], length)
    scores = nt(feat.astype(BF16), key_feat.astype(BF16))
    feat_ref[...] = feat
    kf_ref[...] = key_feat
    lw_ref[...] = jnp.where(causal, scores, 0.0).astype(BF16)
    gain_ref[...] = gl_ref[...]
    sparse_gain_ref[...] = gs_ref[...]
    table_ref[...] = kb_ref[...]


def linear_kernel(
    q_ref, k_ref, v_ref, g_ref, r_ref, feat_ref, kf_ref, lw_ref, gl_ref,
    send_ref, kloc_ref, rg_ref, lg_ref,
):
    keys = k_ref[0]
    values = v_ref[0]
    length, size = keys.shape
    step = r_ref.shape[1]
    queries = stacked(q_ref, size)
    state = whole(r_ref[...])
    slope = jnp.minimum(feat_ref[...], 1.0)
    key_slope = jnp.minimum(kf_ref[...], 1.0)
    feat = feat_ref[...].astype(BF16)
    key_feat = kf_ref[...].astype(BF16)
    upstream = stacked(g_ref, size).astype(F32)
    lin_out = nn(feat, state) + nn(lw_ref[...], values)
    lin_grad = norm_backward(lin_out, upstream * gains(gl_ref, length, size))
    lin_high, lin_low = split(lin_grad)
    causal = causal_mask(queries.shape[0], length)
    score_grad = jnp.where(causal, nt(lin_high, values), 0.0).astype(BF16)
    feat_grad = nt(lin_high, state) + nt(lin_low, state) + nn(score_grad, key_feat)
    raw_grad = (feat_grad * slope).astype(BF16)
    rg_ref[...] = raw_grad
    lg_ref[...] = lin_high
    key_local = tn(score_grad, feat)
    kloc_ref[...] = key_local
    send_ref[:, :step] = pieces(tn(feat, lin_high) + tn(feat, lin_low)).astype(BF16)
    local_high, local_low = split(key_local * key_slope)
    early = tn(raw_grad, queries) + tn(local_high, keys) + tn(local_low, keys)
    send_ref[:, step:] = pieces(early.astype(BF16))


def sparse_kernel(
    q_ref, k_ref, v_ref, g_ref, gs_ref, kb_ref, rk_ref, rv_ref, pf_ref, ps_ref,
    qs_ref, back_ref, dk_ref, dv_ref,
):
    spot, shard = spots()[1:]
    keys = k_ref[0]
    values = v_ref[0]
    length, size = keys.shape
    scaling = size ** (-0.5)
    queries = stacked(q_ref, size)
    upstream = stacked(g_ref, size).astype(F32)
    causal = causal_mask(queries.shape[0], length)
    reaches = kb_ref.shape[1]
    table = kb_ref[0]
    column = lax.broadcasted_iota(jnp.int32, table.shape, 1)
    listed = jnp.max(jnp.where(column == shard, table, -1), axis=1, keepdims=True)
    even = flag(spot % 2 == 0)
    key_far = []
    value_far = []
    live = []
    for reach in range(1, reaches + 1):
        near = jnp.maximum(spot - reach, 0)
        other = jnp.clip(spot - reach + SIDE // 2, 0, SIDE // 2 - 1)
        first = pf_ref[other].astype(F32)
        second = ps_ref[SIDE + other].astype(F32)
        inside = flag(spot >= reach)
        for ref, here, there, out in (
            (rk_ref, first, second, key_far),
            (rv_ref, second, first, value_far),
        ):
            outside = even * here + (1.0 - even) * there
            own = ref[near].astype(F32)
            out.append((inside * own + (1.0 - inside) * outside).astype(BF16))
        here = jnp.where(listed[reach - 1 : reach] >= 0, 1.0, 0.0)
        live.append(jnp.broadcast_to(here, (1, length)))
    key_far = jnp.concatenate(key_far, axis=0)
    value_far = jnp.concatenate(value_far, axis=0)
    live = jnp.concatenate(live, axis=1)
    near_logits = jnp.where(causal, scaling * nt(queries, keys), -jnp.inf)
    far_logits = jnp.where(live > 0.5, scaling * nt(queries, key_far), -jnp.inf)
    top = jnp.maximum(
        jnp.max(near_logits, axis=1, keepdims=True), jnp.max(far_logits, axis=1, keepdims=True)
    )
    near_exp = jnp.exp(near_logits - top)
    far_exp = jnp.exp(far_logits - top)
    norm = 1.0 / (
        jnp.sum(near_exp, axis=1, keepdims=True) + jnp.sum(far_exp, axis=1, keepdims=True)
    )
    near_probs = near_exp * norm
    far_probs = far_exp * norm
    near_half = near_probs.astype(BF16)
    far_half = far_probs.astype(BF16)
    sparse_out = nn(near_half, values) + nn(far_half, value_far)
    sparse_grad = norm_backward(sparse_out, upstream * gains(gs_ref, length, size)).astype(BF16)
    inner = jnp.sum(sparse_grad.astype(F32) * sparse_out, axis=1, keepdims=True)
    near_grad = (scaling * near_probs * (nt(sparse_grad, values) - inner)).astype(BF16)
    far_grad = (scaling * far_probs * (nt(sparse_grad, value_far) - inner)).astype(BF16)
    qs_ref[...] = nn(near_grad, keys) + nn(far_grad, key_far)
    dk_ref[...] = tn(near_grad, queries)
    dv_ref[...] = tn(near_half, sparse_grad)
    key_back = tn(far_grad, queries).astype(BF16)
    value_back = tn(far_half, sparse_grad).astype(BF16)
    for reach in range(reaches):
        part = slice(reach * length, (reach + 1) * length)
        back_ref[reach, :length] = key_back[part]
        back_ref[reach, length:] = value_back[part]


def finish_kernel(w_ref, rg_ref, lg_ref, lw_ref, qs_ref, dv_ref, qo_ref, vo_ref):
    length, size = dv_ref.shape
    query_out = qs_ref[...] + nt(rg_ref[...], w_ref[...])
    for h in range(qs_ref.shape[0] // length):
        qo_ref[0, :, h * size : (h + 1) * size] = query_out[
            h * length : (h + 1) * length
        ].astype(BF16)
    vo_ref[...] = dv_ref[...] + tn(lw_ref[...], lg_ref[...])


def total_kernel(r_ref, o_ref):
    step = o_ref.shape[1]
    total = jnp.sum(r_ref[:, :step].astype(F32), axis=0).astype(BF16)
    for place in range(SIDE):
        o_ref[place] = total


def slope_kernel(half_ref, other_ref, w_ref, slope_ref, rk_ref, rv_ref):
    spot = spots()[1]
    w = w_ref[...]
    step, _ = slope_ref.shape[1:]

    @pl.when(spot % 2 == 0)
    def _():
        rk_ref[...] = half_ref[...]
        rv_ref[...] = other_ref[:SIDE]

    @pl.when(spot % 2 == 1)
    def _():
        rk_ref[...] = other_ref[:SIDE]
        rv_ref[...] = half_ref[...]

    row, col = iotas((step, w.shape[1]))
    own = nt(ones_where(col == row + step * spot), w).astype(BF16)
    for source in range(SIDE):
        slope_ref[source] = features(nt(own, rk_ref[source]))[1]


def weight_part_kernel(
    rk_ref, rv_ref, slope_ref, r_ref, c_ref, own_ref, back_ref,
    send_ref, o_ref, keep_ref, give_ref,
):
    line, spot = spots()[:2]
    step, length = slope_ref.shape[1:]
    total = jnp.zeros(c_ref.shape[1:], F32)
    for source in range(SIDE):
        total = total + flag(source > line) * c_ref[source].astype(F32)
    weight = jnp.sum(r_ref[:, step:].astype(F32), axis=0)
    for source in range(SIDE - 1, -1, -1):
        high, low = split(total)
        o_ref[source] = high
        keys = rk_ref[source]
        values = rv_ref[source]
        slope = slope_ref[source]
        grad_high, grad_low = split((nt(high, values) + nt(low, values)) * slope)
        weight = weight + nn(grad_high, keys) + nn(grad_low, keys)
        total = total + r_ref[source, :step].astype(F32)
    weight = weight.astype(BF16)
    for place in range(SIDE):
        send_ref[place] = weight
    keep_ref[...] = jnp.zeros(keep_ref.shape, BF16)
    give_ref[...] = jnp.zeros(give_ref.shape, BF16)
    for parity, own, other in ((0, keep_ref, give_ref), (1, give_ref, keep_ref)):
        for reach in range(1, own_ref.shape[0] + 1):

            @pl.when((spot % 2 == parity) & (spot >= reach))
            def _():
                own[spot - reach] = own_ref[reach - 1, :length]
                other[spot - reach] = own_ref[reach - 1, length:]

            @pl.when((spot % 2 == parity) & (spot < reach))
            def _():
                own[spot - reach + SIDE] = back_ref[reach - 1, :length]
                other[spot - reach + SIDE] = back_ref[reach - 1, length:]


def column_sum_kernel(r_ref, o_ref):
    total = jnp.sum(r_ref[...].astype(F32), axis=0).astype(BF16)
    for place in range(o_ref.shape[0]):
        o_ref[place] = total


def make_last_kernel(scale):
    def last_kernel(r_ref, carried_ref, keep_ref, got_ref, o_ref):
        step = r_ref.shape[1]
        high, low = split(jnp.sum(r_ref[...].astype(F32), axis=0) * scale)
        o_ref[:, :step] = carried_ref[...]
        for spot in range(SIDE):
            o_ref[spot, step : 2 * step] = high
            o_ref[spot, 2 * step : 3 * step] = low
        for spot in range(SIDE):
            far = keep_ref[spot].astype(F32) + got_ref[spot].astype(F32)
            o_ref[spot, 3 * step :] = far.astype(BF16)

    return last_kernel


def key_kernel(
    k_ref, v_ref, w_ref, r_ref, kloc_ref, dk_ref, dv_ref, ko_ref, vo_ref, wo_ref
):
    keys = k_ref[0]
    values = v_ref[0]
    w = w_ref[...]
    step = w.shape[1] // SIDE
    carried = whole(r_ref[:, :step])
    weight = whole(r_ref[:, step : 2 * step]).astype(F32)
    weight = weight + whole(r_ref[:, 2 * step : 3 * step]).astype(F32)
    wo_ref[...] = weight.T
    key_back, value_back = (
        sum(r_ref[spot, 3 * step :].astype(F32) for spot in range(parity, SIDE, 2))
        for parity in range(2)
    )
    feat, slope = features(nn(keys, w))
    feat = feat.astype(BF16)
    feat_grad = nt(values, carried) + kloc_ref[...]
    raw_grad = (feat_grad * slope).astype(BF16)
    ko_ref[0] = (dk_ref[...] + key_back + nt(raw_grad, w)).astype(BF16)
    vo_ref[0] = (dv_ref[...] + value_back + nn(feat, carried)).astype(BF16)


def call(kernel, *outs, grant=8, space=pltpu.VMEM, scratch=()):
    shapes = [jax.ShapeDtypeStruct(shape, dtype) for shape, dtype in outs]
    spec = pl.BlockSpec(memory_space=pltpu.VMEM)

    def run(*operands):
        return pl.pallas_call(
            kernel,
            out_shape=shapes if len(shapes) > 1 else shapes[0],
            in_specs=[pl.BlockSpec(memory_space=space)] * len(operands),
            out_specs=[spec] * len(shapes) if len(shapes) > 1 else spec,
            scratch_shapes=scratch,
            interpret=INTERPRET,
            compiler_params=pltpu.CompilerParams(vmem_limit_bytes=grant << 20),
        )(*operands)

    return run


def swap(value, axis, groups=None):
    return lax.all_to_all(value, axis, 0, 0, axis_index_groups=groups, tiled=False)


def per_device(queries, keys, values, out_grad, gain_lin, gain_sparse, key_blocks, w_feat):
    shards = lax.axis_size("ctx")
    groups = lax.axis_size("heads")
    length, size = keys.shape[1:]
    features_n = w_feat.shape[1]
    scale = (queries.shape[0] * groups * length * shards) ** (-0.5)
    step = features_n // SIDE
    in_row = [[line * SIDE + spot for spot in range(SIDE)] for line in range(shards // SIDE)]
    in_column = [[line * SIDE + spot for line in range(shards // SIDE)] for spot in range(SIDE)]
    piece = (SIDE, step, size)
    down = [(i, i + SIDE) for i in range(shards - SIDE)]
    rows = (queries.shape[2] // size * length, size)
    square = (length, size)
    single = (SIDE, length, size)
    sent = call(
        send_state_kernel,
        ((SIDE, step + length, size), BF16),
        space=pltpu.HBM,
        scratch=[pltpu.VMEM(item.shape, BF16) for item in (keys, values, w_feat)]
        + [pltpu.SemaphoreType.DMA((3,))],
    )(keys, values, w_feat)
    row = swap(sent, "ctx", in_row)
    sent, own, moved = call(
        row_total_kernel,
        (piece, BF16),
        ((SIDE, length, size), BF16),
        ((SIDE // 2, length, size), BF16),
    )(row)
    got = swap(sent, "ctx", in_column)
    previous = lax.ppermute(moved, "ctx", down)
    twins = [(i, i ^ 1) for i in range(shards)]
    packed = call(pack_kernel, ((3 * SIDE // 2, length, size), BF16))(own, previous)
    other = lax.ppermute(packed, "ctx", twins)
    sent = call(prefix_kernel, (piece, BF16))(row, got)
    got = swap(sent, "ctx", in_row)
    table = jnp.swapaxes(key_blocks, 1, 2)
    *local, sparse_gain, table = call(
        local_kernel,
        ((rows[0], features_n), F32),
        ((length, features_n), F32),
        ((rows[0], length), BF16),
        (gain_lin.shape, F32),
        (gain_sparse.shape, F32),
        (table.shape, table.dtype),
    )(queries, keys, w_feat, gain_lin, gain_sparse, table)
    slopes, row_keys, row_values = call(
        slope_kernel,
        ((SIDE, step, length), F32),
        ((SIDE, length, size), BF16),
        ((SIDE, length, size), BF16),
    )(own, other, w_feat)
    query_sparse, back, key_near, value_near = call(
        sparse_kernel,
        (rows, F32),
        ((key_blocks.shape[2], 2 * length, size), BF16),
        (square, F32),
        (square, F32),
        grant=12,
    )(
        queries, keys, values, out_grad, sparse_gain, table,
        row_keys, row_values, previous, other,
    )
    sent, key_local, raw_grad, lin_grad = call(
        linear_kernel,
        ((SIDE, 2 * step, size), BF16),
        ((length, features_n), F32),
        ((rows[0], features_n), BF16),
        (rows, BF16),
    )(queries, keys, values, out_grad, got, *local)
    cots = swap(sent, "ctx", in_row)
    returned = lax.ppermute(back, "ctx", [(b, a) for a, b in down])
    query_out, value_near = call(finish_kernel, (queries.shape, BF16), (square, F32))(
        w_feat, raw_grad, lin_grad, local[2], query_sparse, value_near
    )
    sent = call(total_kernel, (piece, BF16))(cots)
    got = swap(sent, "ctx", in_column)
    sent, carried, keep, give = call(
        weight_part_kernel, (piece, BF16), (piece, BF16), (single, BF16), (single, BF16)
    )(row_keys, row_values, slopes, cots, got, back, returned)
    taken = lax.ppermute(give, "ctx", [(i, i ^ 1) for i in range(shards)])
    got = swap(sent, "ctx", in_column)
    sent = call(column_sum_kernel, ((groups, step, size), BF16))(got)
    got = swap(sent, "heads")
    sent = call(make_last_kernel(scale), ((SIDE, 3 * step + length, size), BF16))(
        got, carried, keep, taken
    )
    got = swap(sent, "ctx", in_row)
    key_out, value_out, weight = call(
        key_kernel, (keys.shape, BF16), (values.shape, BF16), (w_feat.shape, F32)
    )(keys, values, w_feat, got, key_local, key_near, value_near)
    return query_out, key_out, value_out, weight


def solution(mesh):
    sharded = P("heads", "ctx", None)
    return jax.shard_map(
        per_device,
        mesh=mesh,
        in_specs=(
            sharded,
            sharded,
            sharded,
            sharded,
            P("heads", None),
            P("heads", None),
            P("heads", None, None),
            P(),
        ),
        out_specs=(sharded, sharded, sharded, P()),
        check_vma=False,
    )
```

```python
import jax
import jax.numpy as jnp
from jax import lax
from jax.experimental import pallas as pl
from jax.experimental.pallas import tpu as pltpu
from jax.sharding import PartitionSpec as P


INTERPRET = False
EPS = 1e-06
F32 = jnp.float32
BF16 = jnp.bfloat16


def nn(a, b):
    return lax.dot_general(a, b, (((1,), (0,)), ((), ())), preferred_element_type=F32)


def nt(a, b):
    return lax.dot_general(a, b, (((1,), (1,)), ((), ())), preferred_element_type=F32)


def tn(a, b):
    return lax.dot_general(a, b, (((0,), (0,)), ((), ())), preferred_element_type=F32)


def iotas(shape):
    return (
        lax.broadcasted_iota(jnp.int32, shape, 0),
        lax.broadcasted_iota(jnp.int32, shape, 1),
    )


def ones_where(mask):
    return jnp.where(mask, 1.0, 0.0).astype(BF16)


def features(raw):
    low = jnp.exp(jnp.minimum(raw, 0.0))
    up = raw > 0
    return jnp.where(up, raw + 1.0, low), jnp.where(up, 1.0, low)


def norm_backward(value, upstream):
    inverse = lax.rsqrt(jnp.mean(value * value, axis=-1, keepdims=True) + EPS)
    projected = jnp.mean(upstream * value, axis=-1, keepdims=True)
    return inverse * upstream - value * (inverse * inverse * inverse) * projected


def split(value):
    high = value.astype(BF16)
    return high, (value - high.astype(F32)).astype(BF16)


SIDE = 8


def spots():
    shard = lax.axis_index("ctx")
    return shard // SIDE, shard % SIDE, shard


def flag(condition):
    return jnp.where(condition, 1.0, 0.0).astype(F32)


def pieces(value):
    return value.reshape(SIDE, value.shape[0] // SIDE, value.shape[1])


def whole(value):
    return value.reshape(value.shape[0] * value.shape[1], value.shape[2])


def send_state_kernel(k_hbm, v_hbm, w_hbm, o_ref, k_ref, v_ref, w_ref, sem):
    copies = [
        pltpu.make_async_copy(source, target, sem.at[place])
        for place, (source, target) in enumerate(
            ((k_hbm, k_ref), (v_hbm, v_ref), (w_hbm, w_ref))
        )
    ]
    for copy in copies:
        copy.start()
    for copy in copies:
        copy.wait()
    keys = k_ref[0]
    values = v_ref[0]
    feat = features(nn(keys, w_ref[...]))[0].astype(BF16)
    total = pieces(tn(feat, values).astype(BF16))
    step = total.shape[1]
    o_ref[:, :step] = total
    for spot in range(SIDE):
        o_ref[spot, step:] = values if spot % 2 else keys


def row_total_kernel(r_ref, o_ref, half_ref, moved_ref):
    step = o_ref.shape[1]
    total = jnp.sum(r_ref[:, :step].astype(F32), axis=0).astype(BF16)
    for place in range(SIDE):
        o_ref[place] = total
    half_ref[...] = r_ref[:, step:]
    moved_ref[...] = r_ref[SIDE // 2 :, step:]


def pack_kernel(a_ref, b_ref, o_ref):
    o_ref[:SIDE] = a_ref[...]
    o_ref[SIDE:] = b_ref[...]


def prefix_kernel(r_ref, c_ref, o_ref):
    step = c_ref.shape[1]
    line = spots()[0]
    total = jnp.zeros(c_ref.shape[1:], F32)
    for source in range(SIDE):
        total = total + flag(source < line) * c_ref[source].astype(F32)
    for spot in range(SIDE):
        o_ref[spot] = total.astype(BF16)
        total = total + r_ref[spot, :step].astype(F32)


def stacked(ref, size):
    heads = ref.shape[2] // size
    return jnp.concatenate([ref[0, :, h * size : (h + 1) * size] for h in range(heads)], axis=0)


def gains(ref, length, size):
    heads = ref.shape[1] // size
    return jnp.concatenate(
        [
            jnp.broadcast_to(ref[:, h * size : (h + 1) * size], (length, size))
            for h in range(heads)
        ],
        axis=0,
    )


def causal_mask(rows, length):
    row, col = iotas((rows, length))
    return (row & (length - 1)) >= col


def local_kernel(
    q_ref, k_ref, w_ref, gl_ref, gs_ref, kb_ref,
    feat_ref, kf_ref, lw_ref, gain_ref, sparse_gain_ref, table_ref,
):
    keys = k_ref[0]
    w = w_ref[...]
    length, size = keys.shape
    queries = stacked(q_ref, size)
    feat = features(nn(queries, w))[0]
    key_feat = features(nn(keys, w))[0]
    causal = causal_mask(queries.shape[0], length)
    scores = nt(feat.astype(BF16), key_feat.astype(BF16))
    feat_ref[...] = feat
    kf_ref[...] = key_feat
    lw_ref[...] = jnp.where(causal, scores, 0.0).astype(BF16)
    gain_ref[...] = gl_ref[...]
    sparse_gain_ref[...] = gs_ref[...]
    table_ref[...] = kb_ref[...]


def linear_kernel(
    q_ref, k_ref, v_ref, g_ref, r_ref, feat_ref, kf_ref, lw_ref, gl_ref,
    send_ref, kloc_ref, rg_ref, lg_ref,
):
    keys = k_ref[0]
    values = v_ref[0]
    length, size = keys.shape
    step = r_ref.shape[1]
    queries = stacked(q_ref, size)
    state = whole(r_ref[...])
    slope = jnp.minimum(feat_ref[...], 1.0)
    key_slope = jnp.minimum(kf_ref[...], 1.0)
    feat = feat_ref[...].astype(BF16)
    key_feat = kf_ref[...].astype(BF16)
    upstream = stacked(g_ref, size).astype(F32)
    lin_out = nn(feat, state) + nn(lw_ref[...], values)
    lin_grad = norm_backward(lin_out, upstream * gains(gl_ref, length, size))
    lin_high, lin_low = split(lin_grad)
    causal = causal_mask(queries.shape[0], length)
    score_grad = jnp.where(causal, nt(lin_high, values), 0.0).astype(BF16)
    feat_grad = nt(lin_high, state) + nt(lin_low, state) + nn(score_grad, key_feat)
    raw_grad = (feat_grad * slope).astype(BF16)
    rg_ref[...] = raw_grad
    lg_ref[...] = lin_high
    key_local = tn(score_grad, feat)
    kloc_ref[...] = key_local
    send_ref[:, :step] = pieces(tn(feat, lin_high) + tn(feat, lin_low)).astype(BF16)
    local_high, local_low = split(key_local * key_slope)
    early = tn(raw_grad, queries) + tn(local_high, keys) + tn(local_low, keys)
    send_ref[:, step:] = pieces(early.astype(BF16))


def sparse_kernel(
    q_ref, k_ref, v_ref, g_ref, gs_ref, kb_ref, rk_ref, rv_ref, pf_ref, ps_ref,
    qs_ref, back_ref, dk_ref, dv_ref,
):
    spot, shard = spots()[1:]
    keys = k_ref[0]
    values = v_ref[0]
    length, size = keys.shape
    scaling = size ** (-0.5)
    queries = stacked(q_ref, size)
    upstream = stacked(g_ref, size).astype(F32)
    causal = causal_mask(queries.shape[0], length)
    reaches = kb_ref.shape[1]
    table = kb_ref[0]
    column = lax.broadcasted_iota(jnp.int32, table.shape, 1)
    listed = jnp.max(jnp.where(column == shard, table, -1), axis=1, keepdims=True)
    even = flag(spot % 2 == 0)
    key_far = []
    value_far = []
    live = []
    for reach in range(1, reaches + 1):
        near = jnp.maximum(spot - reach, 0)
        other = jnp.clip(spot - reach + SIDE // 2, 0, SIDE // 2 - 1)
        first = pf_ref[other].astype(F32)
        second = ps_ref[SIDE + other].astype(F32)
        inside = flag(spot >= reach)
        for ref, here, there, out in (
            (rk_ref, first, second, key_far),
            (rv_ref, second, first, value_far),
        ):
            outside = even * here + (1.0 - even) * there
            own = ref[near].astype(F32)
            out.append((inside * own + (1.0 - inside) * outside).astype(BF16))
        here = jnp.where(listed[reach - 1 : reach] >= 0, 1.0, 0.0)
        live.append(jnp.broadcast_to(here, (1, length)))
    key_far = jnp.concatenate(key_far, axis=0)
    value_far = jnp.concatenate(value_far, axis=0)
    live = jnp.concatenate(live, axis=1)
    near_logits = jnp.where(causal, scaling * nt(queries, keys), -jnp.inf)
    far_logits = jnp.where(live > 0.5, scaling * nt(queries, key_far), -jnp.inf)
    top = jnp.maximum(
        jnp.max(near_logits, axis=1, keepdims=True), jnp.max(far_logits, axis=1, keepdims=True)
    )
    near_exp = jnp.exp(near_logits - top)
    far_exp = jnp.exp(far_logits - top)
    norm = 1.0 / (
        jnp.sum(near_exp, axis=1, keepdims=True) + jnp.sum(far_exp, axis=1, keepdims=True)
    )
    near_probs = near_exp * norm
    far_probs = far_exp * norm
    near_half = near_probs.astype(BF16)
    far_half = far_probs.astype(BF16)
    sparse_out = nn(near_half, values) + nn(far_half, value_far)
    sparse_grad = norm_backward(sparse_out, upstream * gains(gs_ref, length, size)).astype(BF16)
    inner = jnp.sum(sparse_grad.astype(F32) * sparse_out, axis=1, keepdims=True)
    near_grad = (scaling * near_probs * (nt(sparse_grad, values) - inner)).astype(BF16)
    far_grad = (scaling * far_probs * (nt(sparse_grad, value_far) - inner)).astype(BF16)
    qs_ref[...] = nn(near_grad, keys) + nn(far_grad, key_far)
    dk_ref[...] = tn(near_grad, queries)
    dv_ref[...] = tn(near_half, sparse_grad)
    key_back = tn(far_grad, queries).astype(BF16)
    value_back = tn(far_half, sparse_grad).astype(BF16)
    for reach in range(reaches):
        part = slice(reach * length, (reach + 1) * length)
        back_ref[reach, :length] = key_back[part]
        back_ref[reach, length:] = value_back[part]


def finish_kernel(w_ref, rg_ref, lg_ref, lw_ref, qs_ref, dv_ref, qo_ref, vo_ref):
    length, size = dv_ref.shape
    query_out = qs_ref[...] + nt(rg_ref[...], w_ref[...])
    for h in range(qs_ref.shape[0] // length):
        qo_ref[0, :, h * size : (h + 1) * size] = query_out[
            h * length : (h + 1) * length
        ].astype(BF16)
    vo_ref[...] = dv_ref[...] + tn(lw_ref[...], lg_ref[...])


def total_kernel(r_ref, o_ref):
    step = o_ref.shape[1]
    total = jnp.sum(r_ref[:, :step].astype(F32), axis=0).astype(BF16)
    for place in range(SIDE):
        o_ref[place] = total


def slope_kernel(half_ref, other_ref, w_ref, slope_ref, rk_ref, rv_ref):
    spot = spots()[1]
    w = w_ref[...]
    step, _ = slope_ref.shape[1:]

    @pl.when(spot % 2 == 0)
    def _():
        rk_ref[...] = half_ref[...]
        rv_ref[...] = other_ref[:SIDE]

    @pl.when(spot % 2 == 1)
    def _():
        rk_ref[...] = other_ref[:SIDE]
        rv_ref[...] = half_ref[...]

    row, col = iotas((step, w.shape[1]))
    own = nt(ones_where(col == row + step * spot), w).astype(BF16)
    for source in range(SIDE):
        slope_ref[source] = features(nt(own, rk_ref[source]))[1]


def weight_part_kernel(
    rk_ref, rv_ref, slope_ref, r_ref, c_ref, own_ref, back_ref,
    send_ref, o_ref, keep_ref, give_ref,
):
    line, spot = spots()[:2]
    step, length = slope_ref.shape[1:]
    total = jnp.zeros(c_ref.shape[1:], F32)
    for source in range(SIDE):
        total = total + flag(source > line) * c_ref[source].astype(F32)
    weight = jnp.sum(r_ref[:, step:].astype(F32), axis=0)
    for source in range(SIDE - 1, -1, -1):
        high, low = split(total)
        o_ref[source] = high
        keys = rk_ref[source]
        values = rv_ref[source]
        slope = slope_ref[source]
        grad_high, grad_low = split((nt(high, values) + nt(low, values)) * slope)
        weight = weight + nn(grad_high, keys) + nn(grad_low, keys)
        total = total + r_ref[source, :step].astype(F32)
    weight = weight.astype(BF16)
    for place in range(SIDE):
        send_ref[place] = weight
    keep_ref[...] = jnp.zeros(keep_ref.shape, BF16)
    give_ref[...] = jnp.zeros(give_ref.shape, BF16)
    for parity, own, other in ((0, keep_ref, give_ref), (1, give_ref, keep_ref)):
        for reach in range(1, own_ref.shape[0] + 1):

            @pl.when((spot % 2 == parity) & (spot >= reach))
            def _():
                own[spot - reach] = own_ref[reach - 1, :length]
                other[spot - reach] = own_ref[reach - 1, length:]

            @pl.when((spot % 2 == parity) & (spot < reach))
            def _():
                own[spot - reach + SIDE] = back_ref[reach - 1, :length]
                other[spot - reach + SIDE] = back_ref[reach - 1, length:]


def column_sum_kernel(r_ref, o_ref):
    total = jnp.sum(r_ref[...].astype(F32), axis=0).astype(BF16)
    for place in range(o_ref.shape[0]):
        o_ref[place] = total


def make_last_kernel(scale):
    def last_kernel(r_ref, carried_ref, keep_ref, got_ref, o_ref):
        step = r_ref.shape[1]
        part = (jnp.sum(r_ref[...].astype(F32), axis=0) * scale).astype(BF16)
        o_ref[:, :step] = carried_ref[...]
        for spot in range(SIDE):
            o_ref[spot, step : 2 * step] = part
        for spot in range(SIDE):
            far = keep_ref[spot].astype(F32) + got_ref[spot].astype(F32)
            o_ref[spot, 2 * step :] = far.astype(BF16)

    return last_kernel


def key_kernel(
    k_ref, v_ref, w_ref, r_ref, kloc_ref, dk_ref, dv_ref, ko_ref, vo_ref, wo_ref
):
    keys = k_ref[0]
    values = v_ref[0]
    w = w_ref[...]
    step = w.shape[1] // SIDE
    carried = whole(r_ref[:, :step])
    weight = whole(r_ref[:, step : 2 * step]).astype(F32)
    wo_ref[...] = weight.T
    key_back, value_back = (
        sum(r_ref[spot, 2 * step :].astype(F32) for spot in range(parity, SIDE, 2))
        for parity in range(2)
    )
    feat, slope = features(nn(keys, w))
    feat = feat.astype(BF16)
    feat_grad = nt(values, carried) + kloc_ref[...]
    raw_grad = (feat_grad * slope).astype(BF16)
    ko_ref[0] = (dk_ref[...] + key_back + nt(raw_grad, w)).astype(BF16)
    vo_ref[0] = (dv_ref[...] + value_back + nn(feat, carried)).astype(BF16)


def call(kernel, *outs, grant=8, space=pltpu.VMEM, scratch=()):
    shapes = [jax.ShapeDtypeStruct(shape, dtype) for shape, dtype in outs]
    spec = pl.BlockSpec(memory_space=pltpu.VMEM)

    def run(*operands):
        return pl.pallas_call(
            kernel,
            out_shape=shapes if len(shapes) > 1 else shapes[0],
            in_specs=[pl.BlockSpec(memory_space=space)] * len(operands),
            out_specs=[spec] * len(shapes) if len(shapes) > 1 else spec,
            scratch_shapes=scratch,
            interpret=INTERPRET,
            compiler_params=pltpu.CompilerParams(vmem_limit_bytes=grant << 20),
        )(*operands)

    return run


def swap(value, axis, groups=None):
    return lax.all_to_all(value, axis, 0, 0, axis_index_groups=groups, tiled=False)


def per_device(queries, keys, values, out_grad, gain_lin, gain_sparse, key_blocks, w_feat):
    shards = lax.axis_size("ctx")
    groups = lax.axis_size("heads")
    length, size = keys.shape[1:]
    features_n = w_feat.shape[1]
    scale = (queries.shape[0] * groups * length * shards) ** (-0.5)
    step = features_n // SIDE
    in_row = [[line * SIDE + spot for spot in range(SIDE)] for line in range(shards // SIDE)]
    in_column = [[line * SIDE + spot for line in range(shards // SIDE)] for spot in range(SIDE)]
    piece = (SIDE, step, size)
    down = [(i, i + SIDE) for i in range(shards - SIDE)]
    rows = (queries.shape[2] // size * length, size)
    square = (length, size)
    single = (SIDE, length, size)
    sent = call(
        send_state_kernel,
        ((SIDE, step + length, size), BF16),
        space=pltpu.HBM,
        scratch=[pltpu.VMEM(item.shape, BF16) for item in (keys, values, w_feat)]
        + [pltpu.SemaphoreType.DMA((3,))],
    )(keys, values, w_feat)
    row = swap(sent, "ctx", in_row)
    sent, own, moved = call(
        row_total_kernel,
        (piece, BF16),
        ((SIDE, length, size), BF16),
        ((SIDE // 2, length, size), BF16),
    )(row)
    got = swap(sent, "ctx", in_column)
    previous = lax.ppermute(moved, "ctx", down)
    twins = [(i, i ^ 1) for i in range(shards)]
    packed = call(pack_kernel, ((3 * SIDE // 2, length, size), BF16))(own, previous)
    other = lax.ppermute(packed, "ctx", twins)
    sent = call(prefix_kernel, (piece, BF16))(row, got)
    got = swap(sent, "ctx", in_row)
    table = jnp.swapaxes(key_blocks, 1, 2)
    *local, sparse_gain, table = call(
        local_kernel,
        ((rows[0], features_n), F32),
        ((length, features_n), F32),
        ((rows[0], length), BF16),
        (gain_lin.shape, F32),
        (gain_sparse.shape, F32),
        (table.shape, table.dtype),
    )(queries, keys, w_feat, gain_lin, gain_sparse, table)
    slopes, row_keys, row_values = call(
        slope_kernel,
        ((SIDE, step, length), F32),
        ((SIDE, length, size), BF16),
        ((SIDE, length, size), BF16),
    )(own, other, w_feat)
    query_sparse, back, key_near, value_near = call(
        sparse_kernel,
        (rows, F32),
        ((key_blocks.shape[2], 2 * length, size), BF16),
        (square, F32),
        (square, F32),
        grant=12,
    )(
        queries, keys, values, out_grad, sparse_gain, table,
        row_keys, row_values, previous, other,
    )
    sent, key_local, raw_grad, lin_grad = call(
        linear_kernel,
        ((SIDE, 2 * step, size), BF16),
        ((length, features_n), F32),
        ((rows[0], features_n), BF16),
        (rows, BF16),
    )(queries, keys, values, out_grad, got, *local)
    cots = swap(sent, "ctx", in_row)
    returned = lax.ppermute(back, "ctx", [(b, a) for a, b in down])
    query_out, value_near = call(finish_kernel, (queries.shape, BF16), (square, F32))(
        w_feat, raw_grad, lin_grad, local[2], query_sparse, value_near
    )
    sent = call(total_kernel, (piece, BF16))(cots)
    got = swap(sent, "ctx", in_column)
    sent, carried, keep, give = call(
        weight_part_kernel, (piece, BF16), (piece, BF16), (single, BF16), (single, BF16)
    )(row_keys, row_values, slopes, cots, got, back, returned)
    taken = lax.ppermute(give, "ctx", [(i, i ^ 1) for i in range(shards)])
    got = swap(sent, "ctx", in_column)
    sent = call(column_sum_kernel, ((groups, step, size), BF16))(got)
    got = swap(sent, "heads")
    sent = call(make_last_kernel(scale), ((SIDE, 2 * step + length, size), BF16))(
        got, carried, keep, taken
    )
    got = swap(sent, "ctx", in_row)
    key_out, value_out, weight = call(
        key_kernel, (keys.shape, BF16), (values.shape, BF16), (w_feat.shape, F32)
    )(keys, values, w_feat, got, key_local, key_near, value_near)
    return query_out, key_out, value_out, weight


def solution(mesh):
    sharded = P("heads", "ctx", None)
    return jax.shard_map(
        per_device,
        mesh=mesh,
        in_specs=(
            sharded,
            sharded,
            sharded,
            sharded,
            P("heads", None),
            P("heads", None),
            P("heads", None, None),
            P(),
        ),
        out_specs=(sharded, sharded, sharded, P()),
        check_vma=False,
    )
```
